256 devices in a mesh: aa: 8 (over x, core), ba: 4 (over y), col: 8 (over z).
Axes of the slice: x: 4, y: 4, z: 8, core: 2. Of those that a mesh axis runs over, the one named last changes fastest.
Arguments:
- r_rows: bfloat16 [131072, 128], P(('aa', 'ba', 'col')), may hold values from -6 to 6
- r_keys: int32 [131072], P(('aa', 'ba', 'col')), may hold values from 0 to 4095
- r_counts: int32 [8192], P(('aa', 'ba', 'col')), may hold values from 0 to 16, as said below
- s_rows: bfloat16 [131072, 128], P(('aa', 'ba', 'col')), may hold values from -6 to 6
- s_keys: int32 [131072], P(('aa', 'ba', 'col')), may hold values from 0 to 4095
- s_counts: int32 [8192], P(('aa', 'ba', 'col')), may hold values from 0 to 16, as said below
- t_rows: bfloat16 [262144, 128], P(('aa', 'ba', 'col')), may hold values from -6 to 6
- t_keys: int32 [262144], P(('aa', 'ba', 'col')), may hold values from 0 to 4095
- t_counts: int32 [16384], P(('aa', 'ba', 'col')), may hold values from 0 to 16, as said below
Outputs:
- joined: bfloat16 [131072, 128], P(('aa', 'ba', 'col'))
The draws below stay inside these ranges and needn't reach their ends.
Inputs may be any that keep to these rules, and one draw needn't show every extreme that they name: `r_counts`: in every draw one destination pair, drawn from the seed, gets 16 live slots from every device. `s_counts`: in every draw one destination pair, drawn from the seed, gets 16 live slots from every device. `t_counts`: in every draw one destination pair, drawn from the seed, gets 16 live slots from every device.
All inputs are finite; a program needn't handle non-finite values.
Results may differ from the reference program's by a relative error of at most 0.001.
Values may be sent and summed in bfloat16 or wider, within the bound.
A program may use at most 64 MiB of HBM per device.

```python
import jax
import jax.numpy as jnp
from jax import lax

W = 128
KEYS = 64
CAP = 16
GROUPS_R = 32
GROUPS_S = 32
GROUPS_T = 64
N_AA = 8
N_BA = 4
N_COL = 8
DEVICES = 256


def counts_draw(key, groups):
    values = jax.random.randint(key, (DEVICES, groups), 0, CAP + 1, dtype=jnp.int32)
    heavy = jax.random.randint(jax.random.fold_in(key, 7), (), 0, groups, dtype=jnp.int32)
    column = jnp.arange(groups, dtype=jnp.int32)[None, :]
    values = jnp.where(column == heavy, CAP, values)
    return values.reshape(DEVICES * groups).astype(jnp.int32)


def draw_r_counts(key, part):
    return counts_draw(jax.random.fold_in(key, 11), GROUPS_R)


def draw_s_counts(key, part):
    return counts_draw(jax.random.fold_in(key, 13), GROUPS_S)


def draw_t_counts(key, part):
    return counts_draw(jax.random.fold_in(key, 17), GROUPS_T)


def plant(array, rng, smallest, high):
    extent = array.shape
    spot = [jax.random.randint(jax.random.fold_in(rng, axis), (), 0, extent[axis]) for axis in range(len(extent))]
    array = array.at[tuple(spot)].set(smallest)
    longest = extent.index(max(extent))
    spot[longest] = (spot[longest] + 1) % extent[longest]
    return array.at[tuple(spot)].set(high)


def block_scale(rng, extent, shards, smallest, high):
    gain, own = 1.0, jax.random.fold_in(rng, 6)
    for axis_at, blocks in shards:
        draws = jnp.exp(jax.random.uniform(jax.random.fold_in(own, axis_at), (blocks,), jnp.float32, smallest / len(shards), high / len(shards)))
        gain = gain * jnp.repeat(draws, extent[axis_at] // blocks).reshape([-1 if axis == axis_at else 1 for axis in range(len(extent))])
    return gain


def scatter_about(own_key, extent, scale, limit, pieces=(), held_as=jnp.bfloat16):
    drawn = scale * jax.random.normal(own_key, extent, jnp.float32)
    if pieces:
        drawn = drawn * block_scale(own_key, extent, pieces, -0.22, 0.18)
    return jnp.clip(drawn, -limit, limit).astype(held_as)


def setup_inputs(seed: int = 0) -> dict:
    splits = jax.random.split(jax.random.key(seed), 10)
    return {
        "r_rows": scatter_about(splits[0], (DEVICES * GROUPS_R * CAP, W), 1.0, 6.0, ((0, 256),)),
        "r_keys": plant(jax.random.randint(splits[1], (DEVICES * GROUPS_R * CAP,), 0, KEYS * KEYS), jax.random.fold_in(splits[1], 1), 0, (KEYS * KEYS) - 1).astype(jnp.int32),
        "r_counts": draw_r_counts(jax.random.fold_in(splits[9], 71), 0),
        "s_rows": scatter_about(splits[3], (DEVICES * GROUPS_S * CAP, W), 1.0, 6.0, ((0, 256),)),
        "s_keys": plant(jax.random.randint(splits[4], (DEVICES * GROUPS_S * CAP,), 0, KEYS * KEYS), jax.random.fold_in(splits[4], 1), 0, (KEYS * KEYS) - 1).astype(jnp.int32),
        "s_counts": draw_s_counts(jax.random.fold_in(splits[9], 71), 0),
        "t_rows": scatter_about(splits[6], (DEVICES * GROUPS_T * CAP, W), 1.0, 6.0, ((0, 256),)),
        "t_keys": plant(jax.random.randint(splits[7], (DEVICES * GROUPS_T * CAP,), 0, KEYS * KEYS), jax.random.fold_in(splits[7], 1), 0, (KEYS * KEYS) - 1).astype(jnp.int32),
        "t_counts": draw_t_counts(jax.random.fold_in(splits[9], 71), 0),
    }


def layout(keys, counts, first_n, second_n):
    groups = first_n * second_n
    slot = jnp.arange(keys.shape[0], dtype=jnp.int32)
    group = slot // CAP % groups
    place = slot % CAP
    live = place < counts[slot // CAP]
    first = group // second_n + first_n * (keys // KEYS)
    second = group % second_n + second_n * (keys % KEYS)
    return (first.astype(jnp.int32), second.astype(jnp.int32), live)

def reference(r_rows, r_keys, r_counts, s_rows, s_keys, s_counts, t_rows, t_keys, t_counts):
    width = r_rows.shape[1]
    key_a = KEYS * N_AA
    key_b = KEYS * N_BA
    key_c = KEYS * N_COL
    r_a, r_b, r_live = layout(r_keys, r_counts, N_AA, N_BA)
    s_b, s_c, s_live = layout(s_keys, s_counts, N_BA, N_COL)
    t_a, t_c, t_live = layout(t_keys, t_counts, N_AA, N_COL)
    s_index = (s_b * key_c + s_c).astype(jnp.int32)
    t_index = (t_a * key_c + t_c).astype(jnp.int32)
    s_weight = s_live.astype(jnp.float32)
    t_weight = t_live.astype(jnp.float32)
    sd = jax.ops.segment_sum(s_rows.astype(jnp.float32) * s_weight[:, None], s_index, key_b * key_c).reshape(key_b, key_c, width)
    scount = jax.ops.segment_sum(s_weight, s_index, key_b * key_c).reshape(key_b, key_c)
    tu = jax.ops.segment_sum(t_rows.astype(jnp.float32) * t_weight[:, None], t_index, key_a * key_c).reshape(key_a, key_c, width)
    tcount = jax.ops.segment_sum(t_weight, t_index, key_a * key_c).reshape(key_a, key_c)
    hi = lax.Precision.HIGHEST
    total = jnp.einsum('ac,bcw->abw', tcount, sd, precision=hi) + jnp.einsum('bc,acw->abw', scount, tu, precision=hi)
    triangles = jnp.einsum('ac,bc->ab', tcount, scount, precision=hi)
    flat = (r_a * key_b + r_b).astype(jnp.int32)
    gathered = total.reshape(key_a * key_b, width)[flat]
    counted = triangles.reshape(key_a * key_b)[flat]
    value = r_rows.astype(jnp.float32) * gathered / jnp.sqrt(1.0 + counted)[:, None]
    return jnp.where(r_live[:, None], value, 0.0).astype(jnp.bfloat16)
```

```python
import jax
import jax.numpy as jnp
from jax import lax
from jax.experimental import pallas as pl
from jax.experimental.pallas import tpu as pltpu
from jax.sharding import PartitionSpec as P

KEYS = 64
CAP = 16
W = 128
MESH = pl.DeviceIdType.MESH
CHUNK = 512
ROWS_G = 520
F32 = jnp.float32
BF16 = jnp.bfloat16


def place():
    aa = lax.axis_index("aa")
    return lax.div(aa, 2), lax.rem(aa, 2), lax.axis_index("ba"), lax.axis_index("col")


def dev(x, core, y, z):
    return (2 * x + core, y, z)


def dev_s(d, z):
    return dev(lax.div(d, 8), lax.rem(lax.div(d, 4), 2), lax.rem(d, 4), z)


def dev_t(d, x):
    return dev(x, lax.rem(lax.div(d, 4), 2), lax.rem(d, 4), lax.div(d, 8))


def dev_r(d, core, y):
    return dev(lax.rem(d, 4), core, y, lax.div(d, 4))


def greet(barrier, count, me, target):
    def one(t, carry):
        pl.semaphore_signal(
            barrier, inc=1, device_id=target(lax.rem(me + t, count)), device_id_type=MESH
        )
        return carry

    lax.fori_loop(1, count, one, 0)


def drain(ref, sem):
    pltpu.make_async_copy(ref, ref, sem).wait()


def dispatch_kernel(
    s_rows, s_keys, t_rows, t_keys, r_rows, r_keys,
    s_all, sk_all, t_all, tk_all, r_held, rk_all,
    a_send, a_recv, ring_send, ring_recv, t_send, t_recv, k_send, k_recv,
):
    x, core, y, z = place()
    cy = core * 4 + y
    me_s = x * 8 + cy
    me_t = z * 8 + cy
    me_r = z * 4 + x

    barrier = pltpu.get_barrier_semaphore()
    greet(barrier, 32, me_s, lambda d: dev_s(d, z))
    greet(barrier, 64, me_t, lambda d: dev_t(d, x))
    greet(barrier, 32, me_r, lambda d: dev_r(d, core, y))
    pl.semaphore_wait(barrier, 31 + 63 + 31)

    def exchange(count, me, target, pairs):
        for src, dst, n in pairs:
            pltpu.make_async_copy(src.at[me], dst.at[me], a_recv.at[n]).start()

        def one(t, carry):
            d = lax.rem(me + t, count)
            for src, dst, n in pairs:
                pltpu.make_async_remote_copy(
                    src_ref=src.at[d], dst_ref=dst.at[me],
                    send_sem=a_send.at[n], recv_sem=a_recv.at[n],
                    device_id=target(d), device_id_type=MESH,
                ).start()
            return carry

        lax.fori_loop(1, count, one, 0)

    exchange(32, me_s, lambda d: dev_s(d, z), ((s_keys, sk_all.at[z], 1), (s_rows, s_all.at[z], 0)))
    exchange(64, me_t, lambda d: dev_t(d, x), ((t_keys, tk_all.at[x], 3), (t_rows, t_all.at[x], 2)))
    exchange(32, me_r, lambda d: dev_r(d, core, y), ((r_keys, rk_all.at[cy], 5), (r_rows, r_held, 4)))

    def ring(step, way):
        at = lax.rem(z + 8 - way * step, 8)
        target = dev(x, core, y, lax.rem(z + 8 + way, 8))
        lane = 0 if way == 1 else 1
        return [
            pltpu.make_async_remote_copy(
                src_ref=ref.at[at], dst_ref=ref.at[at],
                send_sem=ring_send.at[lane, step, n], recv_sem=ring_recv.at[lane, step, n],
                device_id=target, device_id_type=MESH,
            )
            for n, ref in enumerate((sk_all, s_all))
        ]

    def wait_ring(step, way):
        at = lax.rem(z + 8 - way * (step + 1), 8)
        lane = 0 if way == 1 else 1
        for n, ref in enumerate((sk_all, s_all)):
            drain(ref.at[at], ring_recv.at[lane, step, n])

    started = []

    def go(copies):
        for c in copies:
            c.start()
        started.extend(copies)

    drain(sk_all.at[z], a_recv.at[1])
    drain(s_all.at[z], a_recv.at[0])
    go(ring(0, 1))
    go(ring(0, -1))

    drain(tk_all.at[x], a_recv.at[3])
    drain(t_all.at[x], a_recv.at[2])
    for o in (2, 1, 3):
        go([
            pltpu.make_async_remote_copy(
                src_ref=ref.at[x], dst_ref=ref.at[x],
                send_sem=t_send.at[o - 1, n], recv_sem=t_recv.at[o - 1, n],
                device_id=dev(lax.rem(x + o, 4), core, y, z), device_id_type=MESH,
            )
            for n, ref in enumerate((tk_all, t_all))
        ])

    drain(rk_all.at[cy], a_recv.at[5])
    for o in range(1, 8):
        d = lax.rem(cy + o, 8)
        go([
            pltpu.make_async_remote_copy(
                src_ref=rk_all.at[cy], dst_ref=rk_all.at[cy],
                send_sem=k_send.at[o - 1], recv_sem=k_recv.at[o - 1],
                device_id=dev(x, lax.div(d, 4), lax.rem(d, 4), z), device_id_type=MESH,
            )
        ])

    for step in (0, 1, 2):
        wait_ring(step, 1)
        go(ring(step + 1, 1))
        wait_ring(step, -1)
        if step < 2:
            go(ring(step + 1, -1))
    wait_ring(3, 1)

    drain(r_held, a_recv.at[4])
    for o in range(1, 4):
        at = lax.rem(x + 4 - o, 4)
        for n, ref in enumerate((tk_all, t_all)):
            drain(ref.at[at], t_recv.at[o - 1, n])
    for o in range(1, 8):
        drain(rk_all.at[lax.rem(cy + 8 - o, 8)], k_recv.at[o - 1])

    for n, src in ((0, s_rows), (1, s_keys), (2, t_rows), (3, t_keys), (4, r_rows), (5, r_keys)):
        sent = src.at[pl.ds(0, src.shape[0] - 1)]
        drain(sent, a_send.at[n])
    for c in started:
        c.wait_send()


def dispatch(s_rows, s_keys, t_rows, t_keys, r_rows, r_keys):
    spec = pl.BlockSpec(memory_space=pl.ANY)
    dma = pltpu.SemaphoreType.DMA
    out = (
        jax.ShapeDtypeStruct((8, 32, CAP, W), BF16),
        jax.ShapeDtypeStruct((8, 32, 1, 128), jnp.int32),
        jax.ShapeDtypeStruct((4, 64, CAP, W), BF16),
        jax.ShapeDtypeStruct((4, 64, 1, 128), jnp.int32),
        jax.ShapeDtypeStruct((32, CAP, W), BF16),
        jax.ShapeDtypeStruct((8, 32, 1, 128), jnp.int32),
    )
    return pl.pallas_call(
        dispatch_kernel,
        out_shape=out,
        in_specs=[spec] * 6,
        out_specs=(spec,) * 6,
        scratch_shapes=[
            dma((6,)), dma((6,)),
            dma((2, 4, 2)), dma((2, 4, 2)),
            dma((3, 2)), dma((3, 2)),
            dma((7,)), dma((7,)),
        ],
        compiler_params=pltpu.CompilerParams(collective_id=0, has_side_effects=True),
        name="dispatch",
    )(s_rows, s_keys, t_rows, t_keys, r_rows, r_keys)


def key_lanes(ref, i):
    return jnp.concatenate([ref[pl.ds(4 * i + r, 1), :] for r in range(4)], axis=1) - 1


def hot(values):
    rows = lax.broadcasted_iota(jnp.int32, (KEYS, CHUNK), 0)
    return jnp.where(rows == values, 1.0, 0.0).astype(BF16)


def last_dims(a, b, **kw):
    return lax.dot_general(a, b, (((1,), (1,)), ((), ())), preferred_element_type=F32, **kw)


def split3(v):
    top = v.astype(BF16)
    rest = v - top.astype(F32)
    mid = rest.astype(BF16)
    low = (rest - mid.astype(F32)).astype(BF16)
    return top, mid, low


def join_kernel(idx, sk, tk, rk, s_rows, t_rows, g, acc_s, acc_t, lhs, rhs):
    def count(i, carry):
        sc, tc = carry
        ks, kt = key_lanes(sk, i), key_lanes(tk, i)
        sc = sc + last_dims(hot(ks >> 6), hot(ks & 63))
        tc = tc + last_dims(hot(kt >> 6), hot(kt & 63))
        return sc, tc

    zero = jnp.zeros((KEYS, KEYS), F32)
    sc, tc = lax.fori_loop(0, 8, count, (zero, zero))

    def term(keys, rows, cnt, acc):
        acc[...] = jnp.zeros_like(acc)
        high = jnp.floor(cnt * (1.0 / 256.0)) * 256.0
        parts = jnp.where(jnp.max(cnt) >= 256.0, 2, 1)

        def part(p, carry):
            share = jnp.where(p == 0, cnt - high, high).astype(BF16)

            def chunk(i, carry):
                kv = key_lanes(keys, i)
                first, second = kv >> 6, kv & 63
                seen = jnp.dot(share, hot(second), preferred_element_type=F32)
                outer, inner = first >> 2, (first & 3).astype(F32)
                for h in range(16):
                    mask = jnp.where(outer == h, 1.0, 0.0)
                    lhs[64 * h:64 * h + 64, :] = (seen * mask).astype(BF16)
                for r in range(4):
                    line = inner[:, 128 * r:128 * r + 128]
                    side = jnp.transpose(jnp.broadcast_to(line, (128, 128)))
                    block = rows[pl.ds(pl.multiple_of(CHUNK * i + 128 * r, 128), 128), :].astype(F32)
                    for q in range(4):
                        rhs[128 * r:128 * r + 128, 128 * q:128 * q + 128] = jnp.where(
                            side == float(q), block, 0.0
                        ).astype(BF16)
                for m in range(2):
                    got = jnp.dot(
                        lhs[512 * m:512 * m + 512, :], rhs[...], preferred_element_type=F32
                    )
                    for q in range(4):
                        acc[q, 512 * m:512 * m + 512, :] += got[:, 128 * q:128 * q + 128]
                return carry

            return lax.fori_loop(0, 8, chunk, carry)

        lax.fori_loop(0, parts, part, 0)

    term(sk, s_rows, tc, acc_s)
    term(tk, t_rows, sc, acc_t)

    tri = last_dims(sc, tc, precision=lax.Precision.HIGHEST)
    stack = jnp.concatenate(split3(tri), axis=1)

    def gather(o, carry):
        kv = key_lanes(rk, o)
        first = hot(kv >> 6)
        sums = jnp.dot(
            stack, jnp.concatenate([first, first, first], axis=0), preferred_element_type=F32
        )
        line = jnp.sum(sums * hot(kv & 63).astype(F32), axis=0, keepdims=True)
        for r in range(4):
            g[o, 512 + r:513 + r, :] = line[:, 128 * r:128 * r + 128]
        g[o, 516:520, :] = jnp.zeros((4, 128), F32)

        def eight(i, carry):
            for u in range(8):
                at = idx[o * 512 + i * 8 + u]
                one, two = at & 4095, at >> 12
                g[o, pl.ds(i * 8 + u, 1), :] = (
                    acc_s[two_part(one), pl.ds(one & 1023, 1), :]
                    + acc_t[two_part(two), pl.ds(two & 1023, 1), :]
                )
            return carry

        return lax.fori_loop(0, 64, eight, carry)

    def two_part(v):
        return v >> 10

    lax.fori_loop(0, 8, gather, 0)


def join(idx, sk, tk, rk, s_rows, t_rows):
    vm = pl.BlockSpec(memory_space=pltpu.VMEM)
    return pl.pallas_call(
        join_kernel,
        out_shape=jax.ShapeDtypeStruct((8, ROWS_G, W), F32),
        in_specs=[pl.BlockSpec(memory_space=pltpu.SMEM)] + [vm] * 5,
        out_specs=vm,
        scratch_shapes=[
            pltpu.VMEM((4, 1024, W), F32),
            pltpu.VMEM((4, 1024, W), F32),
            pltpu.VMEM((1024, CHUNK), BF16),
            pltpu.VMEM((CHUNK, 4 * W), BF16),
        ],
        compiler_params=pltpu.CompilerParams(vmem_limit_bytes=40 << 20),
        name="join",
    )(idx, sk, tk, rk, s_rows, t_rows)


def finish_kernel(g, rows, keys, out, ra, rb, h, joined, sems, p_send, p_recv, y_send, y_recv):
    x, core, y, z = place()
    me_r = z * 4 + x
    barrier = pltpu.get_barrier_semaphore()
    pl.semaphore_signal(barrier, inc=1, device_id=dev(x, 1 - core, y, z), device_id_type=MESH)
    for o in (1, 2, 3):
        pl.semaphore_signal(
            barrier, inc=1, device_id=dev(x, core, lax.rem(y + o, 4), z), device_id_type=MESH
        )
    greet(barrier, 32, me_r, lambda d: dev_r(d, core, y))
    pl.semaphore_wait(barrier, 1 + 3 + 31)

    order = (2, 1, 3, 0)
    partner = []
    for o in order:
        c = pltpu.make_async_remote_copy(
            src_ref=g.at[(1 - core) * 4 + lax.rem(y + o, 4)], dst_ref=ra.at[o],
            send_sem=p_send.at[o], recv_sem=p_recv.at[o],
            device_id=dev(x, 1 - core, y, z), device_id_type=MESH,
        )
        c.start()
        partner.append(c)
    sent = []
    for n, o in enumerate(order):
        partner[n].wait_recv()
        to = lax.rem(y + o, 4)
        h[o] = g[core * 4 + to] + ra[o]
        if o:
            c = pltpu.make_async_remote_copy(
                src_ref=h.at[o], dst_ref=rb.at[o - 1],
                send_sem=y_send.at[o - 1], recv_sem=y_recv.at[o - 1],
                device_id=dev(x, core, to, z), device_id_type=MESH,
            )
            c.start()
            sent.append(c)
    for c in sent:
        c.wait_recv()
    line = h[0, 512:520, :] + rb[0, 512:520, :] + rb[1, 512:520, :] + rb[2, 512:520, :]
    scale = jnp.where(keys[...] > 0, 1.0 / jnp.sqrt(1.0 + line), 0.0)
    for r in range(4):
        at = pl.ds(128 * r, 128)
        side = jnp.transpose(jnp.broadcast_to(scale[r:r + 1, :], (128, 128)))
        total = h[0, at, :] + rb[0, at, :] + rb[1, at, :] + rb[2, at, :]
        value = rows[at, :].astype(F32) * total * side
        joined[8 * r:8 * r + 8] = value.astype(BF16).reshape(8, CAP, W)

    pltpu.make_async_copy(joined.at[me_r], out.at[me_r], sems.at[1]).start()

    def home(t, carry):
        d = lax.rem(me_r + t, 32)
        pltpu.make_async_remote_copy(
            src_ref=joined.at[d], dst_ref=out.at[me_r],
            send_sem=sems.at[0], recv_sem=sems.at[1],
            device_id=dev_r(d, core, y), device_id_type=MESH,
        ).start()
        return carry

    lax.fori_loop(1, 32, home, 0)
    drain(out, sems.at[1])
    drain(joined.at[pl.ds(0, 31)], sems.at[0])
    for c in partner + sent:
        c.wait_send()


def finish(g, rows, keys):
    vm = pl.BlockSpec(memory_space=pltpu.VMEM)
    dma = pltpu.SemaphoreType.DMA
    return pl.pallas_call(
        finish_kernel,
        out_shape=jax.ShapeDtypeStruct((32, CAP, W), BF16),
        in_specs=[vm] * 3,
        out_specs=pl.BlockSpec(memory_space=pl.ANY),
        scratch_shapes=[
            pltpu.VMEM((4, ROWS_G, W), F32),
            pltpu.VMEM((3, ROWS_G, W), F32),
            pltpu.VMEM((4, ROWS_G, W), F32),
            pltpu.VMEM((32, CAP, W), BF16),
            dma((2,)), dma((4,)), dma((4,)), dma((3,)), dma((3,)),
        ],
        compiler_params=pltpu.CompilerParams(
            collective_id=1, has_side_effects=True, vmem_limit_bytes=40 << 20
        ),
        name="finish",
    )(g, rows, keys)


def lay_keys(keys, counts, seat):
    groups = counts.shape[0]
    spot = lax.broadcasted_iota(jnp.int32, (groups, CAP), 1)
    live = jnp.where(spot < counts[:, None], keys.reshape(groups, CAP) + 1, 0)
    lane = lax.broadcasted_iota(jnp.int32, (groups, 128), 1)
    wide = jnp.where(lane // CAP == seat, jnp.tile(live, (1, 8)), 0)
    return wide.reshape(groups, 1, 128)


def body(r_rows, r_keys, r_counts, s_rows, s_keys, s_counts, t_rows, t_keys, t_counts):
    x, core, y, z = place()
    cy = core * 4 + y
    s_all, sk_all, t_all, tk_all, r_held, rk_all = dispatch(
        s_rows.reshape(32, CAP, W), lay_keys(s_keys, s_counts, cy),
        t_rows.reshape(64, CAP, W), lay_keys(t_keys, t_counts, cy),
        r_rows.reshape(32, CAP, W), lay_keys(r_keys, r_counts, (z * 4 + x) % 8),
    )
    sk = jnp.sum(sk_all.reshape(32, 8, 128), axis=1)
    tk = jnp.sum(tk_all.reshape(32, 8, 128), axis=1)
    rk = jnp.sum(rk_all.reshape(32, 8, 128), axis=1)
    kv = jnp.maximum(rk - 1, 0)
    a, b = kv >> 6, kv & 63
    at_s = (b & 3) * 1024 + (b >> 2) * 64 + a
    at_t = (a & 3) * 1024 + (a >> 2) * 64 + b
    idx = (at_s + at_t * 4096).reshape(4096)
    g = join(idx, sk, tk, rk, s_all.reshape(4096, W), t_all.reshape(4096, W))
    own = lax.dynamic_slice(rk, (cy * 4, 0), (4, 128))
    own = jnp.concatenate([own, jnp.zeros((4, 128), jnp.int32)], axis=0)
    joined = finish(g, r_held.reshape(512, W), own)
    return joined.reshape(512, W)


def solution(mesh):
    rows, line = P(("aa", "ba", "col"), None), P(("aa", "ba", "col"))
    return jax.shard_map(
        body, mesh=mesh, in_specs=(rows, line, line) * 3, out_specs=rows, check_vma=False
    )
```

```python
import jax
import jax.numpy as jnp
from jax import lax
from jax.experimental import pallas as pl
from jax.experimental.pallas import tpu as pltpu
from jax.sharding import PartitionSpec as P

KEYS = 64
CAP = 16
W = 128
MESH = pl.DeviceIdType.MESH
CHUNK = 512
ROWS_G = 520
F32 = jnp.float32
BF16 = jnp.bfloat16


def place():
    aa = lax.axis_index("aa")
    return lax.div(aa, 2), lax.rem(aa, 2), lax.axis_index("ba"), lax.axis_index("col")


def dev(x, core, y, z):
    return (2 * x + core, y, z)


def dev_s(d, z):
    return dev(lax.div(d, 8), lax.rem(lax.div(d, 4), 2), lax.rem(d, 4), z)


def dev_t(d, x):
    return dev(x, lax.rem(lax.div(d, 4), 2), lax.rem(d, 4), lax.div(d, 8))


def dev_r(d, core, y):
    return dev(lax.rem(d, 4), core, y, lax.div(d, 4))


def greet(barrier, count, me, target):
    def one(t, carry):
        pl.semaphore_signal(
            barrier, inc=1, device_id=target(lax.rem(me + t, count)), device_id_type=MESH
        )
        return carry

    lax.fori_loop(1, count, one, 0)


def drain(ref, sem):
    pltpu.make_async_copy(ref, ref, sem).wait()


def push(src, dst, send, recv, target):
    copy = pltpu.make_async_remote_copy(
        src_ref=src, dst_ref=dst, send_sem=send, recv_sem=recv,
        device_id=target, device_id_type=MESH,
    )
    copy.start()
    return copy


def hot(values):
    rows = lax.broadcasted_iota(jnp.int32, (KEYS, CHUNK), 0)
    return jnp.where(rows == values, 1.0, 0.0).astype(BF16)


def last_dims(a, b, **kw):
    return lax.dot_general(a, b, (((1,), (1,)), ((), ())), preferred_element_type=F32, **kw)


def split3(v):
    top = v.astype(BF16)
    rest = v - top.astype(F32)
    mid = rest.astype(BF16)
    low = (rest - mid.astype(F32)).astype(BF16)
    return top, mid, low


def key_line(ref, block, row):
    return jnp.concatenate([ref[block, row + r:row + r + 1, :] for r in range(4)], axis=1) - 1


def product(kv, share, load, acc, lhs, rhs):
    first, second = kv >> 6, kv & 63
    seen = jnp.dot(share, hot(second), preferred_element_type=F32)
    outer, inner = first >> 2, (first & 3).astype(F32)
    for h in range(16):
        mask = jnp.where(outer == h, 1.0, 0.0)
        lhs[64 * h:64 * h + 64, :] = (seen * mask).astype(BF16)
    for r in range(4):
        side = jnp.transpose(jnp.broadcast_to(inner[:, 128 * r:128 * r + 128], (128, 128)))
        block = load(r).astype(F32)
        for q in range(4):
            rhs[128 * r:128 * r + 128, 128 * q:128 * q + 128] = jnp.where(
                side == float(q), block, 0.0
            ).astype(BF16)
    for m in range(2):
        got = jnp.dot(lhs[512 * m:512 * m + 512, :], rhs[...], preferred_element_type=F32)
        for q in range(4):
            at = 1024 * q + 512 * m
            acc[at:at + 512, :] += got[:, 128 * q:128 * q + 128]


def live_keys(keys, counts):
    rows, groups = keys.shape[0], counts.shape[1]
    row = lax.broadcasted_iota(jnp.int32, (rows, groups), 0)
    group = lax.broadcasted_iota(jnp.int32, (rows, groups), 1)
    spread = jnp.where(group // 8 == row, counts.astype(F32), 0.0).astype(BF16)
    group = lax.broadcasted_iota(jnp.int32, (groups, 128), 0)
    lane = lax.broadcasted_iota(jnp.int32, (groups, 128), 1)
    take = jnp.where(group % 8 == lane // CAP, 1.0, 0.0).astype(BF16)
    held = jnp.dot(spread, take, preferred_element_type=F32)
    spot = (lax.broadcasted_iota(jnp.int32, (rows, 128), 1) % CAP).astype(F32)
    return jnp.where(spot < held, keys + 1, 0)


def pack_keys(arrived, me, at):
    lane = lax.broadcasted_iota(jnp.int32, (1, 128), 1) // CAP
    mine = lax.rem(me, 8)
    for r in range(arrived.shape[0] // 8):
        line = jnp.zeros((1, 128), jnp.int32)
        for seat in range(8):
            turned = pltpu.roll(arrived[8 * r + seat], lax.rem(8 + seat - mine, 8) * CAP, 1)
            line = line + jnp.where(lane == seat, turned, 0)
        at[r:r + 1, :] = line


def dispatch_kernel(
    s_rows, s_keys, s_counts, t_rows, t_keys, t_counts, r_keys, r_counts,
    acc_s, acc_t, s_all, t_all, sk_all, tk_all, rk_all, both,
    sk_out, tk_out, rk_out, sk_in, tk_in, rk_in, lhs, rhs,
    a_send, a_recv, ring_send, ring_recv, t_send, t_recv,
    sg_send, sg_recv, tg_send, tg_recv, rg_send, rg_recv,
):
    x, core, y, z = place()
    cy = core * 4 + y
    me_s = x * 8 + cy
    me_t = z * 8 + cy
    me_r = z * 4 + x

    barrier = pltpu.get_barrier_semaphore()
    greet(barrier, 64, me_t, lambda d: dev_t(d, x))
    greet(barrier, 32, me_r, lambda d: dev_r(d, core, y))
    greet(barrier, 32, me_s, lambda d: dev_s(d, z))
    for keys, counts, out in (
        (s_keys, s_counts, sk_out), (t_keys, t_counts, tk_out), (r_keys, r_counts, rk_out)
    ):
        code = live_keys(keys[...], counts[...])
        for r in range(keys.shape[0]):
            out[r] = code[r:r + 1, :]
    acc_s[...] = jnp.zeros_like(acc_s)
    acc_t[...] = jnp.zeros_like(acc_t)
    sk_all[z] = jnp.zeros((8, 128), jnp.int32)
    rk_all[cy] = jnp.zeros((8, 128), jnp.int32)
    pl.semaphore_wait(barrier, 31 + 63 + 31)

    def send_keys(count, me, target, out, dst, n):
        pltpu.make_async_copy(out.at[lax.div(me, 8)], dst.at[me], a_recv.at[n]).start()

        def one(t, carry):
            d = lax.rem(me + t, count)
            push(out.at[lax.div(d, 8)], dst.at[me], a_send.at[n], a_recv.at[n], target(d))
            return carry

        lax.fori_loop(1, count, one, 0)

    def send_rows(count, me, target, src, dst, n):
        pltpu.make_async_copy(src.at[me], dst.at[me], a_recv.at[n]).start()

        def one(t, carry):
            d = lax.rem(me + t, count)
            push(src.at[d], dst.at[me], a_send.at[n], a_recv.at[n], target(d))
            return carry

        lax.fori_loop(1, count, one, 0)

    def to_s(d):
        return dev_s(d, z)

    def to_t(d):
        return dev_t(d, x)

    send_keys(64, me_t, to_t, tk_out, tk_in, 1)
    send_keys(32, me_s, to_s, sk_out, sk_in, 0)
    send_rows(32, me_s, to_s, s_rows, s_all.at[z], 3)
    send_rows(64, me_t, to_t, t_rows, t_all.at[x], 4)
    send_keys(32, me_r, lambda d: dev_r(d, core, y), rk_out, rk_in, 2)

    started = []
    drain(tk_in, a_recv.at[1])
    pack_keys(tk_in, me_t, tk_all.at[x])
    for o in (2, 1, 3):
        started.append(push(
            tk_all.at[x], tk_all.at[x], tg_send.at[o - 1], tg_recv.at[o - 1],
            dev(lax.rem(x + o, 4), core, y, z),
        ))
    drain(sk_in, a_recv.at[0])
    pack_keys(sk_in, me_s, sk_all.at[z])
    for o in (4, 3, 5, 2, 6, 1, 7):
        started.append(push(
            sk_all.at[z], sk_all.at[z], sg_send.at[o - 1], sg_recv.at[o - 1],
            dev(x, core, y, lax.rem(z + o, 8)),
        ))

    def ring(step, way):
        at = lax.rem(z + 8 - way * step, 8)
        lane = 0 if way == 1 else 1
        started.append(push(
            s_all.at[at], s_all.at[at], ring_send.at[lane, step], ring_recv.at[lane, step],
            dev(x, core, y, lax.rem(z + 8 + way, 8)),
        ))

    def ring_in(step, way):
        at = lax.rem(z + 8 - way * (step + 1), 8)
        drain(s_all.at[at], ring_recv.at[0 if way == 1 else 1, step])
        return at

    drain(s_all.at[z], a_recv.at[3])
    ring(0, 1)
    ring(0, -1)

    drain(rk_in, a_recv.at[2])
    pack_keys(rk_in, me_r, rk_all.at[cy])
    for o in range(1, 8):
        d = lax.rem(cy + o, 8)
        started.append(push(
            rk_all.at[cy], rk_all.at[cy], rg_send.at[o - 1], rg_recv.at[o - 1],
            dev(x, lax.div(d, 4), lax.rem(d, 4), z),
        ))
    for o in range(1, 4):
        drain(tk_all.at[lax.rem(x + 4 - o, 4)], tg_recv.at[o - 1])
    for o in range(1, 8):
        drain(sk_all.at[lax.rem(z + 8 - o, 8)], sg_recv.at[o - 1])

    def count_s(i, total):
        kv = key_line(sk_all, i, 0)
        return total + last_dims(hot(kv >> 6), hot(kv & 63))

    def count_t(i, total):
        for half in range(2):
            kv = key_line(tk_all, i, 4 * half)
            total = total + last_dims(hot(kv >> 6), hot(kv & 63))
        return total

    zero = jnp.zeros((KEYS, KEYS), F32)
    sc = lax.fori_loop(0, 8, count_s, zero)
    tc = lax.fori_loop(0, 4, count_t, zero)
    both[0] = sc
    both[1] = tc

    def low(cnt):
        return cnt - jnp.floor(cnt * (1.0 / 256.0)) * 256.0

    s_share, t_share = low(tc).astype(BF16), low(sc).astype(BF16)

    def do_s(at):
        product(
            key_line(sk_all, at, 0), s_share,
            lambda r: s_all[at, 8 * r:8 * r + 8].reshape(128, W), acc_s, lhs, rhs,
        )

    def do_t(at):
        def half(i, carry):
            kv = jnp.concatenate(
                [tk_all[at, pl.ds(4 * i + r, 1), :] for r in range(4)], axis=1
            ) - 1
            product(
                kv, t_share,
                lambda r: t_all[at, pl.ds(32 * i + 8 * r, 8)].reshape(128, W), acc_t, lhs, rhs,
            )
            return carry

        lax.fori_loop(0, 2, half, 0)

    def do_many(spots, do):
        def one(n, carry):
            at = spots[0]
            for k in range(1, len(spots)):
                at = jnp.where(n == k, spots[k], at)
            do(at)
            return carry

        lax.fori_loop(0, len(spots), one, 0)

    drain(t_all.at[x], a_recv.at[4])
    for o in (2, 1, 3):
        started.append(push(
            t_all.at[x], t_all.at[x], t_send.at[o - 1], t_recv.at[o - 1],
            dev(lax.rem(x + o, 4), core, y, z),
        ))
    behind = [z]
    for step in (0, 1, 2):
        got = [ring_in(step, 1)]
        ring(step + 1, 1)
        got.append(ring_in(step, -1))
        if step < 2:
            ring(step + 1, -1)
        do_many(behind, do_s)
        if step == 0:
            do_t(x)
        behind = got
    do_many(behind, do_s)
    do_s(ring_in(3, 1))
    spots = []
    for o in (1, 3, 2):
        at = lax.rem(x + 4 - o, 4)
        drain(t_all.at[at], t_recv.at[o - 1])
        spots.append(at)
    do_many(spots, do_t)

    for o in range(1, 8):
        drain(rk_all.at[lax.rem(cy + 8 - o, 8)], rg_recv.at[o - 1])
    for n, ref in enumerate((sk_in, tk_in, rk_in)):
        drain(ref.at[pl.ds(0, ref.shape[0] - 1)], a_send.at[n])
    for n, ref in ((3, s_rows), (4, t_rows)):
        drain(ref.at[pl.ds(0, ref.shape[0] - 1)], a_send.at[n])
    for c in started:
        c.wait_send()


def dispatch(*args):
    hbm = pl.BlockSpec(memory_space=pl.ANY)
    vm = pl.BlockSpec(memory_space=pltpu.VMEM)
    dma = pltpu.SemaphoreType.DMA
    i32 = jnp.int32
    out = (
        jax.ShapeDtypeStruct((4096, W), F32),
        jax.ShapeDtypeStruct((4096, W), F32),
        jax.ShapeDtypeStruct((8, 32, CAP, W), BF16),
        jax.ShapeDtypeStruct((4, 64, CAP, W), BF16),
        jax.ShapeDtypeStruct((8, 8, 128), i32),
        jax.ShapeDtypeStruct((4, 8, 128), i32),
        jax.ShapeDtypeStruct((8, 8, 128), i32),
        jax.ShapeDtypeStruct((2, KEYS, KEYS), F32),
    )
    return pl.pallas_call(
        dispatch_kernel,
        out_shape=out,
        in_specs=[hbm, vm, vm, hbm, vm, vm, vm, vm],
        out_specs=(vm,) * 8,
        scratch_shapes=[
            pltpu.VMEM((4, 1, 128), i32), pltpu.VMEM((8, 1, 128), i32), pltpu.VMEM((4, 1, 128), i32),
            pltpu.VMEM((32, 1, 128), i32), pltpu.VMEM((64, 1, 128), i32), pltpu.VMEM((32, 1, 128), i32),
            pltpu.VMEM((1024, CHUNK), BF16),
            pltpu.VMEM((CHUNK, 4 * W), BF16),
            dma((5,)), dma((5,)),
            dma((2, 4)), dma((2, 4)),
            dma((3,)), dma((3,)),
            dma((7,)), dma((7,)),
            dma((3,)), dma((3,)),
            dma((7,)), dma((7,)),
        ],
        compiler_params=pltpu.CompilerParams(
            collective_id=0, has_side_effects=True, vmem_limit_bytes=24 << 20
        ),
        name="dispatch",
    )(*args)


def repair_kernel(
    both, sk_all, tk_all, s_all, t_all, was_s, was_t, acc_s, acc_t, block, table, lhs, rhs, sem
):
    @pl.when(jnp.max(both[...]) >= 256.0)
    def _():
        def high(cnt):
            return (jnp.floor(cnt * (1.0 / 256.0)) * 256.0).astype(BF16)

        def move(src, dst):
            copy = pltpu.make_async_copy(src, dst, sem)
            copy.start()
            copy.wait()

        def load(r):
            return block[8 * r:8 * r + 8].reshape(128, W)

        s_share, t_share = high(both[1]), high(both[0])

        def one_s(i, carry):
            move(s_all.at[i], block)
            product(key_line(sk_all, i, 0), s_share, load, table, lhs, rhs)
            return carry

        def one_t(i, carry):
            for half in range(2):
                move(t_all.at[i, pl.ds(32 * half, 32)], block)
                product(key_line(tk_all, i, 4 * half), t_share, load, table, lhs, rhs)
            return carry

        move(was_s, table)
        lax.fori_loop(0, 8, one_s, 0)
        move(table, acc_s)
        move(was_t, table)
        lax.fori_loop(0, 4, one_t, 0)
        move(table, acc_t)


def repair(both, sk_all, tk_all, s_all, t_all, acc_s, acc_t):
    hbm = pl.BlockSpec(memory_space=pl.ANY)
    vm = pl.BlockSpec(memory_space=pltpu.VMEM)
    total = jax.ShapeDtypeStruct((4096, W), F32)
    return pl.pallas_call(
        repair_kernel,
        out_shape=(total, total),
        in_specs=[vm, vm, vm, hbm, hbm, hbm, hbm],
        out_specs=(hbm, hbm),
        input_output_aliases={5: 0, 6: 1},
        scratch_shapes=[
            pltpu.VMEM((32, CAP, W), BF16),
            pltpu.VMEM((4096, W), F32),
            pltpu.VMEM((1024, CHUNK), BF16),
            pltpu.VMEM((CHUNK, 4 * W), BF16),
            pltpu.SemaphoreType.DMA,
        ],
        compiler_params=pltpu.CompilerParams(vmem_limit_bytes=24 << 20),
        name="repair",
    )(both, sk_all, tk_all, s_all, t_all, acc_s, acc_t)


def finish_kernel(
    idx, acc_s, acc_t, rk_all, both, r_rows, out,
    away, ra, rb, h, rows, joined, sems, p_send, p_recv, y_send, y_recv,
):
    x, core, y, z = place()
    me_r = z * 4 + x
    barrier = pltpu.get_barrier_semaphore()
    pl.semaphore_signal(barrier, inc=1, device_id=dev(x, 1 - core, y, z), device_id_type=MESH)
    for o in (1, 2, 3):
        pl.semaphore_signal(
            barrier, inc=1, device_id=dev(x, core, lax.rem(y + o, 4), z), device_id_type=MESH
        )
    greet(barrier, 32, me_r, lambda d: dev_r(d, core, y))

    tri = last_dims(both[0], both[1], precision=lax.Precision.HIGHEST)
    stack = jnp.concatenate(split3(tri), axis=1)

    def gather(o, to):
        kv = jnp.concatenate([rk_all[o, r:r + 1, :] for r in range(4)], axis=1) - 1
        first = hot(kv >> 6)
        sums = jnp.dot(
            stack, jnp.concatenate([first, first, first], axis=0), preferred_element_type=F32
        )
        line = jnp.sum(sums * hot(kv & 63).astype(F32), axis=0, keepdims=True)
        for r in range(4):
            to[512 + r:513 + r, :] = line[:, 128 * r:128 * r + 128]
        to[516:520, :] = jnp.zeros((4, 128), F32)

        def some(i, carry):
            for u in range(16):
                at = idx[o * 512 + i * 16 + u]
                to[pl.ds(i * 16 + u, 1), :] = (
                    acc_s[pl.ds(at & 4095, 1), :] + acc_t[pl.ds(at >> 12, 1), :]
                )
            return carry

        lax.fori_loop(0, 32, some, 0)

    order = (2, 1, 3, 0)
    gather((1 - core) * 4 + lax.rem(y + 2, 4), away.at[2])
    pl.semaphore_wait(barrier, 1 + 3 + 31)

    pltpu.make_async_copy(r_rows.at[me_r], rows.at[me_r], sems.at[3]).start()

    def spread(t, carry):
        d = lax.rem(me_r + t, 32)
        push(r_rows.at[d], rows.at[me_r], sems.at[2], sems.at[3], dev_r(d, core, y))
        return carry

    partner, sent = [], []
    for n, o in enumerate(order):
        to = lax.rem(y + o, 4)
        if n:
            gather((1 - core) * 4 + to, away.at[o])
        partner.append(push(
            away.at[o], ra.at[o], p_send.at[o], p_recv.at[o], dev(x, 1 - core, y, z)
        ))
        if n == 0:
            lax.fori_loop(1, 32, spread, 0)
        gather(core * 4 + to, h.at[o])
        partner[n].wait_recv()
        h[o] = h[o] + ra[o]
        if o:
            sent.append(push(
                h.at[o], rb.at[o - 1], y_send.at[o - 1], y_recv.at[o - 1], dev(x, core, to, z)
            ))
    drain(rows, sems.at[3])
    for c in sent:
        c.wait_recv()
    line = h[0, 512:516, :] + rb[0, 512:516, :] + rb[1, 512:516, :] + rb[2, 512:516, :]
    scale = jnp.where(rk_all[core * 4 + y, 0:4, :] > 0, 1.0 / jnp.sqrt(1.0 + line), 0.0)
    for r in range(4):
        at = pl.ds(128 * r, 128)
        side = jnp.transpose(jnp.broadcast_to(scale[r:r + 1, :], (128, 128)))
        total = h[0, at, :] + rb[0, at, :] + rb[1, at, :] + rb[2, at, :]
        value = rows[8 * r:8 * r + 8].reshape(128, W).astype(F32) * total * side
        joined[8 * r:8 * r + 8] = value.astype(BF16).reshape(8, CAP, W)

    pltpu.make_async_copy(joined.at[me_r], out.at[me_r], sems.at[1]).start()

    def home(t, carry):
        d = lax.rem(me_r + t, 32)
        push(joined.at[d], out.at[me_r], sems.at[0], sems.at[1], dev_r(d, core, y))
        return carry

    lax.fori_loop(1, 32, home, 0)
    drain(out, sems.at[1])
    drain(joined.at[pl.ds(0, 31)], sems.at[0])
    drain(rows.at[pl.ds(0, 31)], sems.at[2])
    for c in partner + sent:
        c.wait_send()


def finish(idx, acc_s, acc_t, rk_all, both, r_rows):
    vm = pl.BlockSpec(memory_space=pltpu.VMEM)
    hbm = pl.BlockSpec(memory_space=pl.ANY)
    dma = pltpu.SemaphoreType.DMA
    return pl.pallas_call(
        finish_kernel,
        out_shape=jax.ShapeDtypeStruct((32, CAP, W), BF16),
        in_specs=[pl.BlockSpec(memory_space=pltpu.SMEM), vm, vm, vm, vm, hbm],
        out_specs=hbm,
        scratch_shapes=[
            pltpu.VMEM((4, ROWS_G, W), F32),
            pltpu.VMEM((4, ROWS_G, W), F32),
            pltpu.VMEM((3, ROWS_G, W), F32),
            pltpu.VMEM((4, ROWS_G, W), F32),
            pltpu.VMEM((32, CAP, W), BF16),
            pltpu.VMEM((32, CAP, W), BF16),
            dma((4,)), dma((4,)), dma((4,)), dma((3,)), dma((3,)),
        ],
        compiler_params=pltpu.CompilerParams(
            collective_id=1, has_side_effects=True, vmem_limit_bytes=24 << 20
        ),
        name="finish",
    )(idx, acc_s, acc_t, rk_all, both, r_rows)


def body(r_rows, r_keys, r_counts, s_rows, s_keys, s_counts, t_rows, t_keys, t_counts):
    acc_s, acc_t, s_all, t_all, sk_all, tk_all, rk_all, both = dispatch(
        s_rows.reshape(32, CAP, W), s_keys.reshape(4, 128), s_counts.reshape(1, 32),
        t_rows.reshape(64, CAP, W), t_keys.reshape(8, 128), t_counts.reshape(1, 64),
        r_keys.reshape(4, 128), r_counts.reshape(1, 32),
    )
    acc_s, acc_t = repair(both, sk_all, tk_all, s_all, t_all, acc_s, acc_t)
    kv = jnp.maximum(rk_all[:, :4] - 1, 0)
    a, b = kv >> 6, kv & 63
    at_s = (b & 3) * 1024 + (b >> 2) * 64 + a
    at_t = (a & 3) * 1024 + (a >> 2) * 64 + b
    idx = (at_s + at_t * 4096).reshape(4096)
    joined = finish(idx, acc_s, acc_t, rk_all, both, r_rows.reshape(32, CAP, W))
    return joined.reshape(512, W)


def solution(mesh):
    rows, line = P(("aa", "ba", "col"), None), P(("aa", "ba", "col"))
    return jax.shard_map(
        body, mesh=mesh, in_specs=(rows, line, line) * 3, out_specs=rows, check_vma=False
    )
```

```python
import jax
import jax.numpy as jnp
from jax import lax
from jax.experimental import pallas as pl
from jax.experimental.pallas import tpu as pltpu
from jax.sharding import PartitionSpec as P

KEYS = 64
CAP = 16
W = 128
MESH = pl.DeviceIdType.MESH
CHUNK = 512
ROWS_G = 520
HALF_G = 256
F32 = jnp.float32
BF16 = jnp.bfloat16


def place():
    aa = lax.axis_index("aa")
    return lax.div(aa, 2), lax.rem(aa, 2), lax.axis_index("ba"), lax.axis_index("col")


def dev(x, core, y, z):
    return (2 * x + core, y, z)


def around(me, count):
    return [me] + [lax.rem(me + k, count) for k in range(1, count)]


def seats(cy):
    return [(d, lax.div(d, 4), lax.rem(d, 4)) for d in around(cy, 8)]


def each_s(x, cy, z, do):
    near = seats(cy)
    for n, xx in enumerate(around(x, 4)):
        for m, (d, core, y) in enumerate(near):
            if n or m:
                do(xx * 8 + d, xx, dev(xx, core, y, z))


def each_t(x, cy, z, do):
    near = seats(cy)
    for d, core, y in near[1:]:
        do(z * 8 + d, z, dev(x, core, y, z))

    def one(t, carry):
        zz = lax.rem(z + t, 8)
        for d, core, y in near:
            do(zz * 8 + d, zz, dev(x, core, y, zz))
        return carry

    lax.fori_loop(1, 8, one, 0)


def each_r(x, core, y, z, do):
    near = around(x, 4)
    for xx in near[1:]:
        do(z * 4 + xx, lax.div(z, 2), dev(xx, core, y, z))

    def one(t, carry):
        zz = lax.rem(z + t, 8)
        for xx in near:
            do(zz * 4 + xx, lax.div(zz, 2), dev(xx, core, y, zz))
        return carry

    lax.fori_loop(1, 8, one, 0)


def greet(barrier):
    def do(d, row, target):
        pl.semaphore_signal(barrier, inc=1, device_id=target, device_id_type=MESH)

    return do


def drain(ref, sem):
    pltpu.make_async_copy(ref, ref, sem).wait()


def push(src, dst, send, recv, target):
    copy = pltpu.make_async_remote_copy(
        src_ref=src, dst_ref=dst, send_sem=send, recv_sem=recv,
        device_id=target, device_id_type=MESH,
    )
    copy.start()
    return copy


def hot(values):
    rows = lax.broadcasted_iota(jnp.int32, (KEYS, CHUNK), 0)
    return jnp.where(rows == values, 1.0, 0.0).astype(BF16)


def last_dims(a, b, **kw):
    return lax.dot_general(a, b, (((1,), (1,)), ((), ())), preferred_element_type=F32, **kw)


def split3(v):
    top = v.astype(BF16)
    rest = v - top.astype(F32)
    mid = rest.astype(BF16)
    low = (rest - mid.astype(F32)).astype(BF16)
    return top, mid, low


def key_line(ref, block, row):
    return jnp.concatenate([ref[block, row + r:row + r + 1, :] for r in range(4)], axis=1) - 1


def product(kv, share, load, acc, lhs, rhs):
    first, second = kv >> 6, kv & 63
    seen = jnp.dot(share, hot(second), preferred_element_type=F32)
    outer, inner = first >> 2, (first & 3).astype(F32)
    for h in range(16):
        mask = jnp.where(outer == h, 1.0, 0.0)
        lhs[64 * h:64 * h + 64, :] = (seen * mask).astype(BF16)
    for r in range(4):
        side = jnp.transpose(jnp.broadcast_to(inner[:, 128 * r:128 * r + 128], (128, 128)))
        block = load(r).astype(F32)
        for q in range(4):
            rhs[128 * r:128 * r + 128, 128 * q:128 * q + 128] = jnp.where(
                side == float(q), block, 0.0
            ).astype(BF16)
    for m in range(2):
        got = jnp.dot(lhs[512 * m:512 * m + 512, :], rhs[...], preferred_element_type=F32)
        for q in range(4):
            at = 1024 * q + 512 * m
            acc[at:at + 512, :] += got[:, 128 * q:128 * q + 128]


def live_keys(keys, counts):
    rows, groups = keys.shape[0], counts.shape[1]
    row = lax.broadcasted_iota(jnp.int32, (rows, groups), 0)
    group = lax.broadcasted_iota(jnp.int32, (rows, groups), 1)
    spread = jnp.where(group // 8 == row, counts.astype(F32), 0.0).astype(BF16)
    group = lax.broadcasted_iota(jnp.int32, (groups, 128), 0)
    lane = lax.broadcasted_iota(jnp.int32, (groups, 128), 1)
    take = jnp.where(group % 8 == lane // CAP, 1.0, 0.0).astype(BF16)
    held = jnp.dot(spread, take, preferred_element_type=F32)
    spot = (lax.broadcasted_iota(jnp.int32, (rows, 128), 1) % CAP).astype(F32)
    return jnp.where(spot < held, keys + 1, 0)


def pack_keys(arrived, me, at):
    lane = lax.broadcasted_iota(jnp.int32, (1, 128), 1) // CAP
    mine = lax.rem(me, 8)
    for r in range(arrived.shape[0] // 8):
        line = jnp.zeros((1, 128), jnp.int32)
        for seat in range(8):
            turned = pltpu.roll(arrived[8 * r + seat], lax.rem(8 + seat - mine, 8) * CAP, 1)
            line = line + jnp.where(lane == seat, turned, 0)
        at[r:r + 1, :] = line


def dispatch_kernel(
    s_rows, s_keys, s_counts, t_rows, t_keys, t_counts, r_keys, r_counts,
    acc_s, acc_t, s_all, t_all, sk_all, tk_all, rk_all, both,
    sk_own, tk_own, rk_own, sc_own, tc_own, rc_own,
    sk_out, tk_out, rk_out, sk_in, tk_in, rk_in, lhs, rhs, own_sems,
    a_send, a_recv, ring_send, ring_recv, t_send, t_recv,
    sg_send, sg_recv, tg_send, tg_recv, rg_send, rg_recv,
):
    x, core, y, z = place()
    cy = core * 4 + y
    me_s = x * 8 + cy
    me_t = z * 8 + cy
    me_r = z * 4 + x

    fetched = [
        pltpu.make_async_copy(src, dst, own_sems.at[n])
        for n, (src, dst) in enumerate((
            (t_keys, tk_own), (t_counts, tc_own), (s_keys, sk_own),
            (s_counts, sc_own), (r_keys, rk_own), (r_counts, rc_own),
        ))
    ]
    for c in fetched:
        c.start()
    barrier = pltpu.get_barrier_semaphore()
    each_t(x, cy, z, greet(barrier))
    each_r(x, core, y, z, greet(barrier))
    each_s(x, cy, z, greet(barrier))
    for c in fetched:
        c.wait()
    for keys, counts, out in (
        (sk_own, sc_own, sk_out), (tk_own, tc_own, tk_out), (rk_own, rc_own, rk_out)
    ):
        code = live_keys(keys[...], counts[...])
        for r in range(keys.shape[0]):
            out[r] = code[r:r + 1, :]
    acc_s[...] = jnp.zeros_like(acc_s)
    acc_t[...] = jnp.zeros_like(acc_t)
    sk_all[z] = jnp.zeros((8, 128), jnp.int32)
    rk_all[cy] = jnp.zeros((8, 128), jnp.int32)
    pl.semaphore_wait(barrier, 31 + 63 + 31)

    def keys_to(out, dst, me, n):
        def do(d, row, target):
            push(out.at[row], dst.at[me], a_send.at[n], a_recv.at[n], target)

        return do

    def rows_to(src, dst, me, n):
        def do(d, row, target):
            push(src.at[d], dst.at[me], a_send.at[n], a_recv.at[n], target)

        return do

    each_t(x, cy, z, keys_to(tk_out, tk_in, me_t, 1))
    each_s(x, cy, z, keys_to(sk_out, sk_in, me_s, 0))
    each_s(x, cy, z, rows_to(s_rows, s_all.at[z], me_s, 3))
    each_t(x, cy, z, rows_to(t_rows, t_all.at[x], me_t, 4))
    for n, src, dst in (
        (0, sk_out.at[x], sk_in.at[me_s]),
        (1, tk_out.at[z], tk_in.at[me_t]),
        (2, rk_out.at[lax.div(z, 2)], rk_in.at[me_r]),
        (3, s_rows.at[me_s], s_all.at[z, me_s]),
        (4, t_rows.at[me_t], t_all.at[x, me_t]),
    ):
        pltpu.make_async_copy(src, dst, a_recv.at[n]).start()
    each_r(x, core, y, z, keys_to(rk_out, rk_in, me_r, 2))

    started = []

    def ring(step, way):
        at = lax.rem(z + 8 - way * step, 8)
        lane = 0 if way == 1 else 1
        started.append(push(
            s_all.at[at], s_all.at[at], ring_send.at[lane, step], ring_recv.at[lane, step],
            dev(x, core, y, lax.rem(z + 8 + way, 8)),
        ))

    def ring_in(step, way):
        at = lax.rem(z + 8 - way * (step + 1), 8)
        drain(s_all.at[at], ring_recv.at[0 if way == 1 else 1, step])
        return at

    def x_half(block, half, way, n):
        part = t_all.at[block, pl.ds(32 * half, 32)]
        started.append(push(
            part, part, t_send.at[n], t_recv.at[n], dev(lax.rem(x + 4 + way, 4), core, y, z)
        ))

    def x_in(block, half, n):
        drain(t_all.at[block, pl.ds(32 * half, 32)], t_recv.at[n])

    drain(s_all.at[z], a_recv.at[3])
    ring(0, 1)
    ring(0, -1)
    drain(tk_in, a_recv.at[1])
    pack_keys(tk_in, me_t, tk_all.at[x])
    for o in (2, 1, 3):
        started.append(push(
            tk_all.at[x], tk_all.at[x], tg_send.at[o - 1], tg_recv.at[o - 1],
            dev(lax.rem(x + o, 4), core, y, z),
        ))
    drain(sk_in, a_recv.at[0])
    pack_keys(sk_in, me_s, sk_all.at[z])
    for o in (4, 3, 5, 2, 6, 1, 7):
        started.append(push(
            sk_all.at[z], sk_all.at[z], sg_send.at[o - 1], sg_recv.at[o - 1],
            dev(x, core, y, lax.rem(z + o, 8)),
        ))
    drain(t_all.at[x], a_recv.at[4])
    x_half(x, 0, 1, 0)
    x_half(x, 1, -1, 1)
    x_half(x, 1, 1, 2)
    x_half(x, 0, -1, 3)
    got = [ring_in(0, 1)]
    ring(1, 1)
    got.append(ring_in(0, -1))
    ring(1, -1)

    drain(rk_in, a_recv.at[2])
    pack_keys(rk_in, me_r, rk_all.at[cy])
    for o in range(1, 8):
        d = lax.rem(cy + o, 8)
        started.append(push(
            rk_all.at[cy], rk_all.at[cy], rg_send.at[o - 1], rg_recv.at[o - 1],
            dev(x, lax.div(d, 4), lax.rem(d, 4), z),
        ))
    for o in range(1, 4):
        drain(tk_all.at[lax.rem(x + 4 - o, 4)], tg_recv.at[o - 1])
    for o in range(1, 8):
        drain(sk_all.at[lax.rem(z + 8 - o, 8)], sg_recv.at[o - 1])

    def count_s(i, total):
        kv = key_line(sk_all, i, 0)
        return total + last_dims(hot(kv >> 6), hot(kv & 63))

    def count_t(i, total):
        for half in range(2):
            kv = key_line(tk_all, i, 4 * half)
            total = total + last_dims(hot(kv >> 6), hot(kv & 63))
        return total

    zero = jnp.zeros((KEYS, KEYS), F32)
    sc = lax.fori_loop(0, 8, count_s, zero)
    tc = lax.fori_loop(0, 4, count_t, zero)
    both[0] = sc
    both[1] = tc

    def low(cnt):
        return cnt - jnp.floor(cnt * (1.0 / 256.0)) * 256.0

    s_share, t_share = low(tc).astype(BF16), low(sc).astype(BF16)

    def do_s(at):
        product(
            key_line(sk_all, at, 0), s_share,
            lambda r: s_all[at, 8 * r:8 * r + 8].reshape(128, W), acc_s, lhs, rhs,
        )

    def do_t(at):
        def half(i, carry):
            kv = jnp.concatenate(
                [tk_all[at, pl.ds(4 * i + r, 1), :] for r in range(4)], axis=1
            ) - 1
            product(
                kv, t_share,
                lambda r: t_all[at, pl.ds(32 * i + 8 * r, 8)].reshape(128, W), acc_t, lhs, rhs,
            )
            return carry

        lax.fori_loop(0, 2, half, 0)

    def do_many(spots, do):
        def one(n, carry):
            at = spots[0]
            for k in range(1, len(spots)):
                at = jnp.where(n == k, spots[k], at)
            do(at)
            return carry

        lax.fori_loop(0, len(spots), one, 0)

    before, after, far = lax.rem(x + 3, 4), lax.rem(x + 1, 4), lax.rem(x + 2, 4)
    do_t(x)
    x_in(before, 0, 0)
    x_half(before, 0, 1, 4)
    x_in(after, 1, 1)
    x_half(after, 1, -1, 5)
    do_s(z)
    later = [ring_in(1, 1)]
    ring(2, 1)
    later.append(ring_in(1, -1))
    ring(2, -1)
    do_many(got, do_s)
    got = [ring_in(2, 1)]
    ring(3, 1)
    x_in(before, 1, 2)
    x_in(after, 0, 3)
    do_many(later, do_s)
    do_many([before, after], do_t)
    got.append(ring_in(2, -1))
    got.append(ring_in(3, 1))
    do_many(got, do_s)
    x_in(far, 0, 4)
    x_in(far, 1, 5)
    do_t(far)

    for o in range(1, 8):
        drain(rk_all.at[lax.rem(cy + 8 - o, 8)], rg_recv.at[o - 1])
    for n, ref in enumerate((sk_in, tk_in, rk_in)):
        drain(ref.at[pl.ds(0, ref.shape[0] - 1)], a_send.at[n])
    for n, ref in ((3, s_rows), (4, t_rows)):
        drain(ref.at[pl.ds(0, ref.shape[0] - 1)], a_send.at[n])
    for c in started:
        c.wait_send()


def dispatch(*args):
    vm = pl.BlockSpec(memory_space=pltpu.VMEM)
    dma = pltpu.SemaphoreType.DMA
    i32 = jnp.int32
    out = (
        jax.ShapeDtypeStruct((4096, W), F32),
        jax.ShapeDtypeStruct((4096, W), F32),
        jax.ShapeDtypeStruct((8, 32, CAP, W), BF16),
        jax.ShapeDtypeStruct((4, 64, CAP, W), BF16),
        jax.ShapeDtypeStruct((8, 8, 128), i32),
        jax.ShapeDtypeStruct((4, 8, 128), i32),
        jax.ShapeDtypeStruct((8, 8, 128), i32),
        jax.ShapeDtypeStruct((2, KEYS, KEYS), F32),
    )
    return pl.pallas_call(
        dispatch_kernel,
        out_shape=out,
        in_specs=[pl.BlockSpec(memory_space=pltpu.HBM)] * 8,
        out_specs=(vm,) * 8,
        scratch_shapes=[
            pltpu.VMEM((4, 128), i32), pltpu.VMEM((8, 128), i32), pltpu.VMEM((4, 128), i32),
            pltpu.VMEM((1, 32), i32), pltpu.VMEM((1, 64), i32), pltpu.VMEM((1, 32), i32),
            pltpu.VMEM((4, 1, 128), i32), pltpu.VMEM((8, 1, 128), i32), pltpu.VMEM((4, 1, 128), i32),
            pltpu.VMEM((32, 1, 128), i32), pltpu.VMEM((64, 1, 128), i32), pltpu.VMEM((32, 1, 128), i32),
            pltpu.VMEM((1024, CHUNK), BF16),
            pltpu.VMEM((CHUNK, 4 * W), BF16),
            dma((6,)),
            dma((5,)), dma((5,)),
            dma((2, 4)), dma((2, 4)),
            dma((6,)), dma((6,)),
            dma((7,)), dma((7,)),
            dma((3,)), dma((3,)),
            dma((7,)), dma((7,)),
        ],
        compiler_params=pltpu.CompilerParams(
            collective_id=0, has_side_effects=True, vmem_limit_bytes=24 << 20
        ),
        name="dispatch",
    )(*(pltpu.with_memory_space_constraint(a, pltpu.HBM) for a in args))


def repair_kernel(
    both, sk_all, tk_all, s_all, t_all, was_s, was_t, acc_s, acc_t, block, table, lhs, rhs, sem
):
    @pl.when(jnp.max(both[...]) >= 256.0)
    def _():
        def high(cnt):
            return (jnp.floor(cnt * (1.0 / 256.0)) * 256.0).astype(BF16)

        def move(src, dst):
            copy = pltpu.make_async_copy(src, dst, sem)
            copy.start()
            copy.wait()

        def load(r):
            return block[8 * r:8 * r + 8].reshape(128, W)

        s_share, t_share = high(both[1]), high(both[0])

        def one_s(i, carry):
            move(s_all.at[i], block)
            product(key_line(sk_all, i, 0), s_share, load, table, lhs, rhs)
            return carry

        def one_t(i, carry):
            for half in range(2):
                move(t_all.at[i, pl.ds(32 * half, 32)], block)
                product(key_line(tk_all, i, 4 * half), t_share, load, table, lhs, rhs)
            return carry

        move(was_s, table)
        lax.fori_loop(0, 8, one_s, 0)
        move(table, acc_s)
        move(was_t, table)
        lax.fori_loop(0, 4, one_t, 0)
        move(table, acc_t)


def repair(both, sk_all, tk_all, s_all, t_all, acc_s, acc_t):
    hbm = pl.BlockSpec(memory_space=pl.ANY)
    vm = pl.BlockSpec(memory_space=pltpu.VMEM)
    total = jax.ShapeDtypeStruct((4096, W), F32)
    return pl.pallas_call(
        repair_kernel,
        out_shape=(total, total),
        in_specs=[vm, vm, vm, hbm, hbm, hbm, hbm],
        out_specs=(hbm, hbm),
        input_output_aliases={5: 0, 6: 1},
        scratch_shapes=[
            pltpu.VMEM((32, CAP, W), BF16),
            pltpu.VMEM((4096, W), F32),
            pltpu.VMEM((1024, CHUNK), BF16),
            pltpu.VMEM((CHUNK, 4 * W), BF16),
            pltpu.SemaphoreType.DMA,
        ],
        compiler_params=pltpu.CompilerParams(vmem_limit_bytes=24 << 20),
        name="repair",
    )(both, sk_all, tk_all, s_all, t_all, acc_s, acc_t)


def finish_kernel(
    idx, acc_s, acc_t, rk_all, both, r_rows, out,
    away, ra, rb, h, rows, joined, sems, p_send, p_recv, y_send, y_recv,
):
    x, core, y, z = place()
    me_r = z * 4 + x
    barrier = pltpu.get_barrier_semaphore()
    pl.semaphore_signal(barrier, inc=1, device_id=dev(x, 1 - core, y, z), device_id_type=MESH)
    for o in (1, 2, 3):
        pl.semaphore_signal(
            barrier, inc=1, device_id=dev(x, core, lax.rem(y + o, 4), z), device_id_type=MESH
        )
    each_r(x, core, y, z, greet(barrier))

    tri = last_dims(both[0], both[1], precision=lax.Precision.HIGHEST)
    stack = jnp.concatenate(split3(tri), axis=1)

    def gather(o, to):
        kv = jnp.concatenate([rk_all[o, r:r + 1, :] for r in range(4)], axis=1) - 1
        first = hot(kv >> 6)
        sums = jnp.dot(
            stack, jnp.concatenate([first, first, first], axis=0), preferred_element_type=F32
        )
        line = jnp.sum(sums * hot(kv & 63).astype(F32), axis=0, keepdims=True)
        for r in range(4):
            to[512 + r:513 + r, :] = line[:, 128 * r:128 * r + 128]
        to[516:520, :] = jnp.zeros((4, 128), F32)

        def some(i, carry):
            for u in range(16):
                at = idx[o * 512 + i * 16 + u]
                to[pl.ds(i * 16 + u, 1), :] = (
                    acc_s[pl.ds(at & 4095, 1), :] + acc_t[pl.ds(at >> 12, 1), :]
                )
            return carry

        lax.fori_loop(0, 32, some, 0)

    up, down = dev(x, core, lax.rem(y + 1, 4), z), dev(x, core, lax.rem(y + 3, 4), z)
    top, low = pl.ds(0, HALF_G), pl.ds(HALF_G, ROWS_G - HALF_G)

    def theirs(o):
        return (1 - core) * 4 + lax.rem(y + o, 4)

    def spread(d, row, target):
        push(r_rows.at[d], rows.at[me_r], sems.at[2], sems.at[3], target)

    partner, sent = {}, []

    def to_partner(o):
        partner[o] = push(
            away.at[o], ra.at[o], p_send.at[o], p_recv.at[o], dev(x, 1 - core, y, z)
        )

    def meet(o):
        gather(core * 4 + lax.rem(y + o, 4), h.at[o])
        partner[o].wait_recv()
        h[o] = h[o] + ra[o]

    def to_y(src, dst, n, target):
        sent.append(push(src, dst, y_send.at[n], y_recv.at[n], target))

    gather(theirs(2), away.at[2])
    pl.semaphore_wait(barrier, 1 + 3 + 31)
    to_partner(2)
    gather(theirs(1), away.at[1])
    to_partner(1)
    meet(2)
    to_y(h.at[2, top], rb.at[2, top], 0, up)
    to_y(h.at[2, low], rb.at[2, low], 1, down)
    gather(theirs(3), away.at[3])
    to_partner(3)
    meet(1)
    to_y(h.at[1, low], rb.at[0, low], 2, up)
    gather(theirs(0), away.at[0])
    to_partner(0)
    meet(3)
    to_y(h.at[3, top], rb.at[1, top], 3, down)
    drain(rb.at[2, top], y_recv.at[0])
    h[1, top, :] = h[1, top, :] + rb[2, top, :]
    to_y(h.at[1, top], rb.at[0, top], 4, up)
    drain(rb.at[2, low], y_recv.at[1])
    h[3, low, :] = h[3, low, :] + rb[2, low, :]
    to_y(h.at[3, low], rb.at[1, low], 5, down)
    pltpu.make_async_copy(r_rows.at[me_r], rows.at[me_r], sems.at[3]).start()
    each_r(x, core, y, z, spread)
    meet(0)
    drain(rows, sems.at[3])
    for n, part in ((2, rb.at[0, low]), (3, rb.at[1, top]), (4, rb.at[0, top]), (5, rb.at[1, low])):
        drain(part, y_recv.at[n])
    line = h[0, 512:516, :] + rb[0, 512:516, :] + rb[1, 512:516, :]
    scale = jnp.where(rk_all[core * 4 + y, 0:4, :] > 0, 1.0 / jnp.sqrt(1.0 + line), 0.0)
    for r in range(4):
        at = pl.ds(128 * r, 128)
        side = jnp.transpose(jnp.broadcast_to(scale[r:r + 1, :], (128, 128)))
        total = h[0, at, :] + rb[0, at, :] + rb[1, at, :]
        value = rows[8 * r:8 * r + 8].reshape(128, W).astype(F32) * total * side
        joined[8 * r:8 * r + 8] = value.astype(BF16).reshape(8, CAP, W)

    pltpu.make_async_copy(joined.at[me_r], out.at[me_r], sems.at[1]).start()

    def home(d, row, target):
        push(joined.at[d], out.at[me_r], sems.at[0], sems.at[1], target)

    each_r(x, core, y, z, home)
    drain(out, sems.at[1])
    drain(joined.at[pl.ds(0, 31)], sems.at[0])
    drain(rows.at[pl.ds(0, 31)], sems.at[2])
    for c in list(partner.values()) + sent:
        c.wait_send()


def finish(idx, acc_s, acc_t, rk_all, both, r_rows):
    vm = pl.BlockSpec(memory_space=pltpu.VMEM)
    hbm = pl.BlockSpec(memory_space=pltpu.HBM)
    dma = pltpu.SemaphoreType.DMA
    return pl.pallas_call(
        finish_kernel,
        out_shape=jax.ShapeDtypeStruct((32, CAP, W), BF16),
        in_specs=[pl.BlockSpec(memory_space=pltpu.SMEM), vm, vm, vm, vm, hbm],
        out_specs=hbm,
        scratch_shapes=[
            pltpu.VMEM((4, ROWS_G, W), F32),
            pltpu.VMEM((4, ROWS_G, W), F32),
            pltpu.VMEM((3, ROWS_G, W), F32),
            pltpu.VMEM((4, ROWS_G, W), F32),
            pltpu.VMEM((32, CAP, W), BF16),
            pltpu.VMEM((32, CAP, W), BF16),
            dma((4,)), dma((4,)), dma((4,)), dma((6,)), dma((6,)),
        ],
        compiler_params=pltpu.CompilerParams(
            collective_id=1, has_side_effects=True, vmem_limit_bytes=24 << 20
        ),
        name="finish",
    )(idx, acc_s, acc_t, rk_all, both, pltpu.with_memory_space_constraint(r_rows, pltpu.HBM))


def body(r_rows, r_keys, r_counts, s_rows, s_keys, s_counts, t_rows, t_keys, t_counts):
    acc_s, acc_t, s_all, t_all, sk_all, tk_all, rk_all, both = dispatch(
        s_rows.reshape(32, CAP, W), s_keys.reshape(4, 128), s_counts.reshape(1, 32),
        t_rows.reshape(64, CAP, W), t_keys.reshape(8, 128), t_counts.reshape(1, 64),
        r_keys.reshape(4, 128), r_counts.reshape(1, 32),
    )
    acc_s, acc_t = repair(both, sk_all, tk_all, s_all, t_all, acc_s, acc_t)
    kv = jnp.maximum(rk_all[:, :4] - 1, 0)
    a, b = kv >> 6, kv & 63
    at_s = (b & 3) * 1024 + (b >> 2) * 64 + a
    at_t = (a & 3) * 1024 + (a >> 2) * 64 + b
    idx = (at_s + at_t * 4096).reshape(4096)
    joined = finish(idx, acc_s, acc_t, rk_all, both, r_rows.reshape(32, CAP, W))
    return joined.reshape(512, W)


def solution(mesh):
    rows, line = P(("aa", "ba", "col"), None), P(("aa", "ba", "col"))
    return jax.shard_map(
        body, mesh=mesh, in_specs=(rows, line, line) * 3, out_specs=rows, check_vma=False
    )
```

```python
import jax
import jax.numpy as jnp
from jax import lax
from jax.experimental import pallas as pl
from jax.experimental.pallas import tpu as pltpu
from jax.sharding import PartitionSpec as P

KEYS = 64
CAP = 16
W = 128
MESH = pl.DeviceIdType.MESH
CHUNK = 512
ROWS_G = 520
HALF_G = 256
F32 = jnp.float32
BF16 = jnp.bfloat16


def place():
    aa = lax.axis_index("aa")
    return lax.div(aa, 2), lax.rem(aa, 2), lax.axis_index("ba"), lax.axis_index("col")


def dev(x, core, y, z):
    return (2 * x + core, y, z)


def around(me, count):
    return [me] + [lax.rem(me + k, count) for k in range(1, count)]


def seats(cy):
    return [(d, lax.div(d, 4), lax.rem(d, 4)) for d in around(cy, 8)]


def each_s(x, cy, z, do):
    near = seats(cy)
    for n, xx in enumerate(around(x, 4)):
        for m, (d, core, y) in enumerate(near):
            if n or m:
                do(xx * 8 + d, xx, dev(xx, core, y, z))


def each_t(x, cy, z, do):
    near = seats(cy)
    for d, core, y in near[1:]:
        do(z * 8 + d, z, dev(x, core, y, z))

    def one(t, carry):
        zz = lax.rem(z + t, 8)
        for d, core, y in near:
            do(zz * 8 + d, zz, dev(x, core, y, zz))
        return carry

    lax.fori_loop(1, 8, one, 0)


def each_r(x, core, y, z, do):
    near = around(x, 4)
    for xx in near[1:]:
        do(z * 4 + xx, lax.div(z, 2), dev(xx, core, y, z))

    def one(t, carry):
        zz = lax.rem(z + t, 8)
        for xx in near:
            do(zz * 4 + xx, lax.div(zz, 2), dev(xx, core, y, zz))
        return carry

    lax.fori_loop(1, 8, one, 0)


def greet(barrier):
    def do(d, row, target):
        pl.semaphore_signal(barrier, inc=1, device_id=target, device_id_type=MESH)

    return do


def drain(ref, sem):
    pltpu.make_async_copy(ref, ref, sem).wait()


def push(src, dst, send, recv, target):
    copy = pltpu.make_async_remote_copy(
        src_ref=src, dst_ref=dst, send_sem=send, recv_sem=recv,
        device_id=target, device_id_type=MESH,
    )
    copy.start()
    return copy


def hot(values):
    rows = lax.broadcasted_iota(jnp.int32, (KEYS, values.shape[1]), 0)
    return jnp.where(rows == values, 1.0, 0.0).astype(BF16)


def last_dims(a, b, **kw):
    return lax.dot_general(a, b, (((1,), (1,)), ((), ())), preferred_element_type=F32, **kw)


def split3(v):
    top = v.astype(BF16)
    rest = v - top.astype(F32)
    mid = rest.astype(BF16)
    low = (rest - mid.astype(F32)).astype(BF16)
    return top, mid, low


def key_line(ref, block, row):
    return jnp.concatenate([ref[block, row + r:row + r + 1, :] for r in range(4)], axis=1) - 1


def product(kv, share, load, acc, lhs, rhs):
    first, second = kv >> 6, kv & 63
    seen = jnp.dot(share, hot(second), preferred_element_type=F32)
    outer, inner = first >> 2, (first & 3).astype(F32)
    for h in range(16):
        mask = jnp.where(outer == h, 1.0, 0.0)
        lhs[64 * h:64 * h + 64, :] = (seen * mask).astype(BF16)
    for r in range(kv.shape[1] // 128):
        side = jnp.transpose(jnp.broadcast_to(inner[:, 128 * r:128 * r + 128], (128, 128)))
        block = load(r).astype(F32)
        for q in range(4):
            rhs[128 * r:128 * r + 128, 128 * q:128 * q + 128] = jnp.where(
                side == float(q), block, 0.0
            ).astype(BF16)
    for m in range(2):
        got = jnp.dot(lhs[512 * m:512 * m + 512, :], rhs[...], preferred_element_type=F32)
        for q in range(4):
            at = 1024 * q + 512 * m
            acc[at:at + 512, :] += got[:, 128 * q:128 * q + 128]


def live_keys(keys, counts):
    rows, groups = keys.shape[0], counts.shape[1]
    row = lax.broadcasted_iota(jnp.int32, (rows, groups), 0)
    group = lax.broadcasted_iota(jnp.int32, (rows, groups), 1)
    spread = jnp.where(group // 8 == row, counts.astype(F32), 0.0).astype(BF16)
    group = lax.broadcasted_iota(jnp.int32, (groups, 128), 0)
    lane = lax.broadcasted_iota(jnp.int32, (groups, 128), 1)
    take = jnp.where(group % 8 == lane // CAP, 1.0, 0.0).astype(BF16)
    held = jnp.dot(spread, take, preferred_element_type=F32)
    spot = (lax.broadcasted_iota(jnp.int32, (rows, 128), 1) % CAP).astype(F32)
    return jnp.where(spot < held, keys + 1, 0)


def pack_keys(arrived, me, at):
    lane = lax.broadcasted_iota(jnp.int32, (1, 128), 1) // CAP
    mine = lax.rem(me, 8)
    for r in range(arrived.shape[0] // 8):
        line = jnp.zeros((1, 128), jnp.int32)
        for seat in range(8):
            turned = pltpu.roll(arrived[8 * r + seat], lax.rem(8 + seat - mine, 8) * CAP, 1)
            line = line + jnp.where(lane == seat, turned, 0)
        at[r:r + 1, :] = line


def dispatch_kernel(
    s_rows, s_keys, s_counts, t_rows, t_keys, t_counts, r_keys, r_counts,
    acc_s, acc_t, s_all, t_all, sk_all, tk_all, rk_all, both,
    sk_own, tk_own, rk_own, sc_own, tc_own, rc_own,
    sk_out, tk_out, rk_out, sk_in, tk_in, rk_in, lhs, rhs, own_sems,
    a_send, a_recv, ring_send, ring_recv, t_send, t_recv,
    sg_send, sg_recv, tg_send, tg_recv, rg_send, rg_recv,
):
    x, core, y, z = place()
    cy = core * 4 + y
    me_s = x * 8 + cy
    me_t = z * 8 + cy
    me_r = z * 4 + x

    fetched = [
        pltpu.make_async_copy(src, dst, own_sems.at[n])
        for n, (src, dst) in enumerate((
            (t_keys, tk_own), (t_counts, tc_own), (s_keys, sk_own),
            (s_counts, sc_own), (r_keys, rk_own), (r_counts, rc_own),
        ))
    ]
    for c in fetched:
        c.start()
    barrier = pltpu.get_barrier_semaphore()
    each_t(x, cy, z, greet(barrier))
    each_r(x, core, y, z, greet(barrier))
    each_s(x, cy, z, greet(barrier))
    for c in fetched:
        c.wait()
    for keys, counts, out in (
        (sk_own, sc_own, sk_out), (tk_own, tc_own, tk_out), (rk_own, rc_own, rk_out)
    ):
        code = live_keys(keys[...], counts[...])
        for r in range(keys.shape[0]):
            out[r] = code[r:r + 1, :]
    acc_s[...] = jnp.zeros_like(acc_s)
    acc_t[...] = jnp.zeros_like(acc_t)
    sk_all[z] = jnp.zeros((8, 128), jnp.int32)
    rk_all[cy] = jnp.zeros((8, 128), jnp.int32)
    pl.semaphore_wait(barrier, 31 + 63 + 31)

    def keys_to(out, dst, me, n):
        def do(d, row, target):
            push(out.at[row], dst.at[me], a_send.at[n], a_recv.at[n], target)

        return do

    def rows_to(src, dst, me, n):
        def do(d, row, target):
            push(src.at[d], dst.at[me], a_send.at[n], a_recv.at[n], target)

        return do

    each_t(x, cy, z, keys_to(tk_out, tk_in, me_t, 1))
    each_s(x, cy, z, keys_to(sk_out, sk_in, me_s, 0))
    each_s(x, cy, z, rows_to(s_rows, s_all.at[z], me_s, 3))
    each_t(x, cy, z, rows_to(t_rows, t_all.at[x], me_t, 4))
    for n, src, dst in (
        (0, sk_out.at[x], sk_in.at[me_s]),
        (1, tk_out.at[z], tk_in.at[me_t]),
        (2, rk_out.at[lax.div(z, 2)], rk_in.at[me_r]),
        (3, s_rows.at[me_s], s_all.at[z, me_s]),
        (4, t_rows.at[me_t], t_all.at[x, me_t]),
    ):
        pltpu.make_async_copy(src, dst, a_recv.at[n]).start()

    each_r(x, core, y, z, keys_to(rk_out, rk_in, me_r, 2))

    started = []

    def ring(step, way, half):
        at = s_all.at[lax.rem(z + 8 - way * step, 8), pl.ds(16 * half, 16)]
        lane = 0 if way == 1 else 1
        started.append(push(
            at, at, ring_send.at[lane, step, half], ring_recv.at[lane, step, half],
            dev(x, core, y, lax.rem(z + 8 + way, 8)),
        ))

    def relay(step, way, last=False):
        at = lax.rem(z + 8 - way * (step + 1), 8)
        for half in range(2):
            drain(
                s_all.at[at, pl.ds(16 * half, 16)],
                ring_recv.at[0 if way == 1 else 1, step, half],
            )
            if not last:
                ring(step + 1, way, half)
        return at

    def x_half(block, half, way, n):
        part = t_all.at[block, pl.ds(32 * half, 32)]
        started.append(push(
            part, part, t_send.at[n], t_recv.at[n], dev(lax.rem(x + 4 + way, 4), core, y, z)
        ))

    def x_in(block, half, n):
        drain(t_all.at[block, pl.ds(32 * half, 32)], t_recv.at[n])

    drain(s_all.at[z], a_recv.at[3])
    for half in range(2):
        ring(0, 1, half)
        ring(0, -1, half)
    drain(tk_in, a_recv.at[1])
    pack_keys(tk_in, me_t, tk_all.at[x])
    for o in (2, 1, 3):
        started.append(push(
            tk_all.at[x], tk_all.at[x], tg_send.at[o - 1], tg_recv.at[o - 1],
            dev(lax.rem(x + o, 4), core, y, z),
        ))
    drain(sk_in, a_recv.at[0])
    pack_keys(sk_in, me_s, sk_all.at[z])
    for o in (4, 3, 5, 2, 6, 1, 7):
        started.append(push(
            sk_all.at[z], sk_all.at[z], sg_send.at[o - 1], sg_recv.at[o - 1],
            dev(x, core, y, lax.rem(z + o, 8)),
        ))
    one, two = relay(0, 1), relay(0, -1)
    drain(t_all.at[x], a_recv.at[4])
    x_half(x, 0, 1, 0)
    x_half(x, 1, -1, 1)
    x_half(x, 1, 1, 2)
    x_half(x, 0, -1, 3)
    drain(rk_in, a_recv.at[2])
    pack_keys(rk_in, me_r, rk_all.at[cy])
    for o in range(1, 8):
        d = lax.rem(cy + o, 8)
        started.append(push(
            rk_all.at[cy], rk_all.at[cy], rg_send.at[o - 1], rg_recv.at[o - 1],
            dev(x, lax.div(d, 4), lax.rem(d, 4), z),
        ))
    for o in range(1, 4):
        drain(tk_all.at[lax.rem(x + 4 - o, 4)], tg_recv.at[o - 1])
    for o in range(1, 8):
        drain(sk_all.at[lax.rem(z + 8 - o, 8)], sg_recv.at[o - 1])

    def count_s(i, total):
        kv = key_line(sk_all, i, 0)
        return total + last_dims(hot(kv >> 6), hot(kv & 63))

    def count_t(i, total):
        for half in range(2):
            kv = key_line(tk_all, i, 4 * half)
            total = total + last_dims(hot(kv >> 6), hot(kv & 63))
        return total

    zero = jnp.zeros((KEYS, KEYS), F32)
    sc = lax.fori_loop(0, 8, count_s, zero)
    tc = lax.fori_loop(0, 4, count_t, zero)
    both[0] = sc
    both[1] = tc

    def low(cnt):
        return cnt - jnp.floor(cnt * (1.0 / 256.0)) * 256.0

    s_share, t_share = low(tc).astype(BF16), low(sc).astype(BF16)

    def do_s(first, second):
        spots = (first, second)
        kv = jnp.concatenate([key_line(sk_all, at, 0) for at in spots], axis=1)
        product(
            kv, s_share,
            lambda r: s_all[spots[r // 4], 8 * (r % 4):8 * (r % 4) + 8].reshape(128, W),
            acc_s, lhs, rhs,
        )

    def do_t(at):
        kv = jnp.concatenate([key_line(tk_all, at, 0), key_line(tk_all, at, 4)], axis=1)
        product(
            kv, t_share, lambda r: t_all[at, 8 * r:8 * r + 8].reshape(128, W), acc_t, lhs, rhs
        )

    do_s(z, one)
    three, four = relay(1, 1), relay(1, -1)
    do_s(two, three)
    do_t(x)
    before, after, far = lax.rem(x + 3, 4), lax.rem(x + 1, 4), lax.rem(x + 2, 4)
    x_in(before, 0, 0)
    x_half(before, 0, 1, 4)
    x_in(after, 1, 1)
    x_half(after, 1, -1, 5)
    five, six = relay(2, 1), relay(2, -1, True)
    do_s(four, five)
    x_in(before, 1, 2)
    do_t(before)
    x_in(after, 0, 3)
    do_t(after)
    do_s(six, relay(3, 1, True))
    x_in(far, 0, 4)
    x_in(far, 1, 5)
    do_t(far)

    for o in range(1, 8):
        drain(rk_all.at[lax.rem(cy + 8 - o, 8)], rg_recv.at[o - 1])
    for n, ref in enumerate((sk_in, tk_in, rk_in)):
        drain(ref.at[pl.ds(0, ref.shape[0] - 1)], a_send.at[n])
    for n, ref in ((3, s_rows), (4, t_rows)):
        drain(ref.at[pl.ds(0, ref.shape[0] - 1)], a_send.at[n])
    for c in started:
        c.wait_send()


def dispatch(*args):
    vm = pl.BlockSpec(memory_space=pltpu.VMEM)
    dma = pltpu.SemaphoreType.DMA
    i32 = jnp.int32
    out = (
        jax.ShapeDtypeStruct((4096, W), F32),
        jax.ShapeDtypeStruct((4096, W), F32),
        jax.ShapeDtypeStruct((8, 32, CAP, W), BF16),
        jax.ShapeDtypeStruct((4, 64, CAP, W), BF16),
        jax.ShapeDtypeStruct((8, 8, 128), i32),
        jax.ShapeDtypeStruct((4, 8, 128), i32),
        jax.ShapeDtypeStruct((8, 8, 128), i32),
        jax.ShapeDtypeStruct((2, KEYS, KEYS), F32),
    )
    return pl.pallas_call(
        dispatch_kernel,
        out_shape=out,
        in_specs=[pl.BlockSpec(memory_space=pltpu.HBM)] * 8,
        out_specs=(vm,) * 8,
        scratch_shapes=[
            pltpu.VMEM((4, 128), i32), pltpu.VMEM((8, 128), i32), pltpu.VMEM((4, 128), i32),
            pltpu.VMEM((1, 32), i32), pltpu.VMEM((1, 64), i32), pltpu.VMEM((1, 32), i32),
            pltpu.VMEM((4, 1, 128), i32), pltpu.VMEM((8, 1, 128), i32), pltpu.VMEM((4, 1, 128), i32),
            pltpu.VMEM((32, 1, 128), i32), pltpu.VMEM((64, 1, 128), i32), pltpu.VMEM((32, 1, 128), i32),
            pltpu.VMEM((1024, 2 * CHUNK), BF16),
            pltpu.VMEM((2 * CHUNK, 4 * W), BF16),
            dma((6,)),
            dma((5,)), dma((5,)),
            dma((2, 4, 2)), dma((2, 4, 2)),
            dma((6,)), dma((6,)),
            dma((7,)), dma((7,)),
            dma((3,)), dma((3,)),
            dma((7,)), dma((7,)),
        ],
        compiler_params=pltpu.CompilerParams(
            collective_id=0, has_side_effects=True, vmem_limit_bytes=24 << 20
        ),
        name="dispatch",
    )(*(pltpu.with_memory_space_constraint(a, pltpu.HBM) for a in args))


def repair_kernel(
    both, sk_all, tk_all, s_all, t_all, was_s, was_t, acc_s, acc_t, block, table, lhs, rhs, sem
):
    @pl.when(jnp.max(both[...]) >= 256.0)
    def _():
        def high(cnt):
            return (jnp.floor(cnt * (1.0 / 256.0)) * 256.0).astype(BF16)

        def move(src, dst):
            copy = pltpu.make_async_copy(src, dst, sem)
            copy.start()
            copy.wait()

        def load(r):
            return block[8 * r:8 * r + 8].reshape(128, W)

        s_share, t_share = high(both[1]), high(both[0])

        def one_s(i, carry):
            move(s_all.at[i], block)
            product(key_line(sk_all, i, 0), s_share, load, table, lhs, rhs)
            return carry

        def one_t(i, carry):
            for half in range(2):
                move(t_all.at[i, pl.ds(32 * half, 32)], block)
                product(key_line(tk_all, i, 4 * half), t_share, load, table, lhs, rhs)
            return carry

        move(was_s, table)
        lax.fori_loop(0, 8, one_s, 0)
        move(table, acc_s)
        move(was_t, table)
        lax.fori_loop(0, 4, one_t, 0)
        move(table, acc_t)


def repair(both, sk_all, tk_all, s_all, t_all, acc_s, acc_t):
    hbm = pl.BlockSpec(memory_space=pl.ANY)
    vm = pl.BlockSpec(memory_space=pltpu.VMEM)
    total = jax.ShapeDtypeStruct((4096, W), F32)
    return pl.pallas_call(
        repair_kernel,
        out_shape=(total, total),
        in_specs=[vm, vm, vm, hbm, hbm, hbm, hbm],
        out_specs=(hbm, hbm),
        input_output_aliases={5: 0, 6: 1},
        scratch_shapes=[
            pltpu.VMEM((32, CAP, W), BF16),
            pltpu.VMEM((4096, W), F32),
            pltpu.VMEM((1024, CHUNK), BF16),
            pltpu.VMEM((CHUNK, 4 * W), BF16),
            pltpu.SemaphoreType.DMA,
        ],
        compiler_params=pltpu.CompilerParams(vmem_limit_bytes=24 << 20),
        name="repair",
    )(both, sk_all, tk_all, s_all, t_all, acc_s, acc_t)


def finish_kernel(
    idx, acc_s, acc_t, rk_all, both, r_rows, out,
    away, ra, rb, h, scales, rows, joined, sems, p_send, p_recv, y_send, y_recv,
):
    x, core, y, z = place()
    me_r = z * 4 + x
    barrier = pltpu.get_barrier_semaphore()
    pl.semaphore_signal(barrier, inc=1, device_id=dev(x, 1 - core, y, z), device_id_type=MESH)
    for o in (1, 2, 3):
        pl.semaphore_signal(
            barrier, inc=1, device_id=dev(x, core, lax.rem(y + o, 4), z), device_id_type=MESH
        )
    each_r(x, core, y, z, greet(barrier))

    tri = last_dims(both[0], both[1], precision=lax.Precision.HIGHEST)
    stack = jnp.concatenate(split3(tri), axis=1)

    def lines(o, to):
        kv = jnp.concatenate([rk_all[o, r:r + 1, :] for r in range(4)], axis=1) - 1
        first = hot(kv >> 6)
        sums = jnp.dot(
            stack, jnp.concatenate([first, first, first], axis=0), preferred_element_type=F32
        )
        line = jnp.sum(sums * hot(kv & 63).astype(F32), axis=0, keepdims=True)
        for r in range(4):
            to[512 + r:513 + r, :] = line[:, 128 * r:128 * r + 128]
        to[516:520, :] = jnp.zeros((4, 128), F32)

    def gather(o, to):
        def some(i, carry):
            for u in range(16):
                at = idx[o * 512 + i * 16 + u]
                to[pl.ds(i * 16 + u, 1), :] = (
                    acc_s[pl.ds(at & 4095, 1), :] + acc_t[pl.ds(at >> 12, 1), :]
                )
            return carry

        lax.fori_loop(0, 32, some, 0)

    up, down = dev(x, core, lax.rem(y + 1, 4), z), dev(x, core, lax.rem(y + 3, 4), z)
    top, low = pl.ds(0, HALF_G), pl.ds(HALF_G, ROWS_G - HALF_G)

    def theirs(o):
        return (1 - core) * 4 + lax.rem(y + o, 4)

    def mine(o):
        return core * 4 + lax.rem(y + o, 4)

    def spread(d, row, target):
        push(r_rows.at[d], rows.at[me_r], sems.at[2], sems.at[3], target)

    partner, sent = {}, []

    def to_partner(o):
        partner[o] = push(
            away.at[o], ra.at[o], p_send.at[o], p_recv.at[o], dev(x, 1 - core, y, z)
        )

    def meet(o):
        partner[o].wait_recv()
        h[o] = h[o] + ra[o]

    def to_y(src, dst, n, target):
        sent.append(push(src, dst, y_send.at[n], y_recv.at[n], target))

    def both_lines(o, carry):
        lines(theirs(o), away.at[o])
        lines(mine(o), h.at[o])
        return carry

    gather(theirs(2), away.at[2])
    lax.fori_loop(0, 4, both_lines, 0)
    gather(mine(2), h.at[2])
    gather(theirs(1), away.at[1])
    pl.semaphore_wait(barrier, 1 + 3 + 31)
    to_partner(2)
    to_partner(1)
    gather(theirs(3), away.at[3])
    to_partner(3)
    meet(2)
    to_y(h.at[2, top], rb.at[2, top], 0, up)
    to_y(h.at[2, low], rb.at[2, low], 1, down)
    gather(mine(1), h.at[1])
    meet(1)
    to_y(h.at[1, low], rb.at[0, low], 2, up)
    gather(mine(3), h.at[3])
    meet(3)
    to_y(h.at[3, top], rb.at[1, top], 3, down)
    gather(theirs(0), away.at[0])
    to_partner(0)
    drain(rb.at[2, top], y_recv.at[0])
    h[1, top, :] = h[1, top, :] + rb[2, top, :]
    to_y(h.at[1, top], rb.at[0, top], 4, up)
    drain(rb.at[2, low], y_recv.at[1])
    h[3, low, :] = h[3, low, :] + rb[2, low, :]
    to_y(h.at[3, low], rb.at[1, low], 5, down)
    pltpu.make_async_copy(r_rows.at[me_r], rows.at[me_r], sems.at[3]).start()
    each_r(x, core, y, z, spread)
    gather(mine(0), h.at[0])
    meet(0)
    drain(rows, sems.at[3])
    for n, part in ((2, rb.at[0, low]), (3, rb.at[1, top]), (4, rb.at[0, top]), (5, rb.at[1, low])):
        drain(part, y_recv.at[n])
    line = h[0, 512:516, :] + rb[0, 512:516, :] + rb[1, 512:516, :]
    scale = jnp.where(rk_all[core * 4 + y, 0:4, :] > 0, 1.0 / jnp.sqrt(1.0 + line), 0.0)
    scales[...] = scale
    pair = lax.div(z, 2)
    xs = around(x, 4)
    for k in (2, 1, 3, 0):
        r = lax.rem(pair + k, 4)
        at = pl.ds(pl.multiple_of(128 * r, 128), 128)
        spot = pl.ds(8 * r, 8)
        side = jnp.transpose(jnp.broadcast_to(scales[pl.ds(r, 1), :], (128, 128)))
        total = h[0, at, :] + rb[0, at, :] + rb[1, at, :]
        value = rows[spot].reshape(128, W).astype(F32) * total * side
        joined[spot] = value.astype(BF16).reshape(8, CAP, W)
        for zz in (4 * r + 1 - z, z) if k == 0 else (2 * r, 2 * r + 1):
            for n, xx in enumerate(xs):
                d = zz * 4 + xx
                if k == 0 and zz is z and n == 0:
                    pltpu.make_async_copy(joined.at[d], out.at[me_r], sems.at[1]).start()
                else:
                    push(
                        joined.at[d], out.at[me_r], sems.at[0], sems.at[1], dev(xx, core, y, zz)
                    )
    drain(out, sems.at[1])
    drain(joined.at[pl.ds(0, 31)], sems.at[0])
    drain(rows.at[pl.ds(0, 31)], sems.at[2])
    for c in list(partner.values()) + sent:
        c.wait_send()


def finish(idx, acc_s, acc_t, rk_all, both, r_rows):
    vm = pl.BlockSpec(memory_space=pltpu.VMEM)
    hbm = pl.BlockSpec(memory_space=pltpu.HBM)
    dma = pltpu.SemaphoreType.DMA
    return pl.pallas_call(
        finish_kernel,
        out_shape=jax.ShapeDtypeStruct((32, CAP, W), BF16),
        in_specs=[pl.BlockSpec(memory_space=pltpu.SMEM), vm, vm, vm, vm, hbm],
        out_specs=hbm,
        scratch_shapes=[
            pltpu.VMEM((4, ROWS_G, W), F32),
            pltpu.VMEM((4, ROWS_G, W), F32),
            pltpu.VMEM((3, ROWS_G, W), F32),
            pltpu.VMEM((4, ROWS_G, W), F32),
            pltpu.VMEM((4, 128), F32),
            pltpu.VMEM((32, CAP, W), BF16),
            pltpu.VMEM((32, CAP, W), BF16),
            dma((4,)), dma((4,)), dma((4,)), dma((6,)), dma((6,)),
        ],
        compiler_params=pltpu.CompilerParams(
            collective_id=1, has_side_effects=True, vmem_limit_bytes=24 << 20
        ),
        name="finish",
    )(idx, acc_s, acc_t, rk_all, both, pltpu.with_memory_space_constraint(r_rows, pltpu.HBM))


def body(r_rows, r_keys, r_counts, s_rows, s_keys, s_counts, t_rows, t_keys, t_counts):
    acc_s, acc_t, s_all, t_all, sk_all, tk_all, rk_all, both = dispatch(
        s_rows.reshape(32, CAP, W), s_keys.reshape(4, 128), s_counts.reshape(1, 32),
        t_rows.reshape(64, CAP, W), t_keys.reshape(8, 128), t_counts.reshape(1, 64),
        r_keys.reshape(4, 128), r_counts.reshape(1, 32),
    )
    acc_s, acc_t = repair(both, sk_all, tk_all, s_all, t_all, acc_s, acc_t)
    kv = jnp.maximum(rk_all[:, :4] - 1, 0)
    a, b = kv >> 6, kv & 63
    at_s = (b & 3) * 1024 + (b >> 2) * 64 + a
    at_t = (a & 3) * 1024 + (a >> 2) * 64 + b
    idx = (at_s + at_t * 4096).reshape(4096)
    joined = finish(idx, acc_s, acc_t, rk_all, both, r_rows.reshape(32, CAP, W))
    return joined.reshape(512, W)


def solution(mesh):
    rows, line = P(("aa", "ba", "col"), None), P(("aa", "ba", "col"))
    return jax.shard_map(
        body, mesh=mesh, in_specs=(rows, line, line) * 3, out_specs=rows, check_vma=False
    )
```

```python
import jax
import jax.numpy as jnp
from jax import lax
from jax.experimental import pallas as pl
from jax.experimental.pallas import tpu as pltpu
from jax.sharding import PartitionSpec as P

KEYS = 64
CAP = 16
W = 128
MESH = pl.DeviceIdType.MESH
CHUNK = 512
ROWS_G = 520
HALF_G = 256
F32 = jnp.float32
BF16 = jnp.bfloat16


def place():
    aa = lax.axis_index("aa")
    return lax.div(aa, 2), lax.rem(aa, 2), lax.axis_index("ba"), lax.axis_index("col")


def dev(x, core, y, z):
    return (2 * x + core, y, z)


def around(me, count):
    return [me] + [lax.rem(me + k, count) for k in range(1, count)]


def seats(cy):
    return [(d, lax.div(d, 4), lax.rem(d, 4)) for d in around(cy, 8)]


def each_s(x, cy, z, do):
    near = seats(cy)
    for n, xx in enumerate(around(x, 4)):
        for m, (d, core, y) in enumerate(near):
            if n or m:
                do(xx * 8 + d, xx, dev(xx, core, y, z))


def each_t(x, cy, z, do):
    near = seats(cy)
    for d, core, y in near[1:]:
        do(z * 8 + d, z, dev(x, core, y, z))

    def one(t, carry):
        zz = lax.rem(z + t, 8)
        for d, core, y in near:
            do(zz * 8 + d, zz, dev(x, core, y, zz))
        return carry

    lax.fori_loop(1, 8, one, 0)


def each_r(x, core, y, z, do):
    near = around(x, 4)
    for xx in near[1:]:
        do(z * 4 + xx, lax.div(z, 2), dev(xx, core, y, z))

    def one(t, carry):
        zz = lax.rem(z + t, 8)
        for xx in near:
            do(zz * 4 + xx, lax.div(zz, 2), dev(xx, core, y, zz))
        return carry

    lax.fori_loop(1, 8, one, 0)


def greet(barrier):
    def do(d, row, target):
        pl.semaphore_signal(barrier, inc=1, device_id=target, device_id_type=MESH)

    return do


def drain(ref, sem):
    pltpu.make_async_copy(ref, ref, sem).wait()


def push(src, dst, send, recv, target):
    copy = pltpu.make_async_remote_copy(
        src_ref=src, dst_ref=dst, send_sem=send, recv_sem=recv,
        device_id=target, device_id_type=MESH,
    )
    copy.start()
    return copy


def hot(values):
    rows = lax.broadcasted_iota(jnp.int32, (KEYS, values.shape[1]), 0)
    return jnp.where(rows == values, 1.0, 0.0).astype(BF16)


def last_dims(a, b, **kw):
    return lax.dot_general(a, b, (((1,), (1,)), ((), ())), preferred_element_type=F32, **kw)


def split3(v):
    top = v.astype(BF16)
    rest = v - top.astype(F32)
    mid = rest.astype(BF16)
    low = (rest - mid.astype(F32)).astype(BF16)
    return top, mid, low


def key_line(ref, block, row):
    return jnp.concatenate([ref[block, row + r:row + r + 1, :] for r in range(4)], axis=1) - 1


def product(kv, share, load, acc, lhs, rhs):
    first, second = kv >> 6, kv & 63
    seen = jnp.dot(share, hot(second), preferred_element_type=F32)
    outer, inner = first >> 2, (first & 3).astype(F32)
    for h in range(16):
        mask = jnp.where(outer == h, 1.0, 0.0)
        lhs[64 * h:64 * h + 64, :] = (seen * mask).astype(BF16)
    for r in range(kv.shape[1] // 128):
        side = jnp.transpose(jnp.broadcast_to(inner[:, 128 * r:128 * r + 128], (128, 128)))
        block = load(r).astype(F32)
        for q in range(4):
            rhs[128 * r:128 * r + 128, 128 * q:128 * q + 128] = jnp.where(
                side == float(q), block, 0.0
            ).astype(BF16)
    for m in range(2):
        got = jnp.dot(lhs[512 * m:512 * m + 512, :], rhs[...], preferred_element_type=F32)
        for q in range(4):
            at = 1024 * q + 512 * m
            acc[at:at + 512, :] += got[:, 128 * q:128 * q + 128]


def live_keys(keys, counts):
    rows, groups = keys.shape[0], counts.shape[1]
    row = lax.broadcasted_iota(jnp.int32, (rows, groups), 0)
    group = lax.broadcasted_iota(jnp.int32, (rows, groups), 1)
    spread = jnp.where(group // 8 == row, counts.astype(F32), 0.0).astype(BF16)
    group = lax.broadcasted_iota(jnp.int32, (groups, 128), 0)
    lane = lax.broadcasted_iota(jnp.int32, (groups, 128), 1)
    take = jnp.where(group % 8 == lane // CAP, 1.0, 0.0).astype(BF16)
    held = jnp.dot(spread, take, preferred_element_type=F32)
    spot = (lax.broadcasted_iota(jnp.int32, (rows, 128), 1) % CAP).astype(F32)
    return jnp.where(spot < held, keys + 1, 0)


def pack_keys(arrived, me, at):
    lane = lax.broadcasted_iota(jnp.int32, (1, 128), 1) // CAP
    mine = lax.rem(me, 8)
    for r in range(arrived.shape[0] // 8):
        line = jnp.zeros((1, 128), jnp.int32)
        for seat in range(8):
            turned = pltpu.roll(arrived[8 * r + seat], lax.rem(8 + seat - mine, 8) * CAP, 1)
            line = line + jnp.where(lane == seat, turned, 0)
        at[r:r + 1, :] = line


def dispatch_kernel(
    s_rows, s_keys, s_counts, t_rows, t_keys, t_counts, r_keys, r_counts,
    acc_s, acc_t, s_all, t_all, sk_all, tk_all, rk_all, both,
    sk_own, tk_own, rk_own, sc_own, tc_own, rc_own,
    sk_out, tk_out, rk_out, sk_in, tk_in, rk_in, lhs, rhs, own_sems,
    a_send, a_recv, ring_send, ring_recv, t_send, t_recv,
    sg_send, sg_recv, tg_send, tg_recv, rg_send, rg_recv,
):
    x, core, y, z = place()
    cy = core * 4 + y
    me_s = x * 8 + cy
    me_t = z * 8 + cy
    me_r = z * 4 + x

    fetched = [
        pltpu.make_async_copy(src, dst, own_sems.at[n])
        for n, (src, dst) in enumerate((
            (t_keys, tk_own), (t_counts, tc_own), (s_keys, sk_own),
            (s_counts, sc_own), (r_keys, rk_own), (r_counts, rc_own),
        ))
    ]
    for c in fetched:
        c.start()
    barrier = pltpu.get_barrier_semaphore()
    each_t(x, cy, z, greet(barrier))
    each_r(x, core, y, z, greet(barrier))
    each_s(x, cy, z, greet(barrier))
    for c in fetched:
        c.wait()
    for keys, counts, out in (
        (sk_own, sc_own, sk_out), (tk_own, tc_own, tk_out), (rk_own, rc_own, rk_out)
    ):
        code = live_keys(keys[...], counts[...])
        for r in range(keys.shape[0]):
            out[r] = code[r:r + 1, :]
    acc_s[...] = jnp.zeros_like(acc_s)
    acc_t[...] = jnp.zeros_like(acc_t)
    sk_all[z] = jnp.zeros((8, 128), jnp.int32)
    rk_all[cy] = jnp.zeros((8, 128), jnp.int32)
    pl.semaphore_wait(barrier, 31 + 63 + 31)

    def keys_to(out, dst, me, n):
        def do(d, row, target):
            push(out.at[row], dst.at[me], a_send.at[n], a_recv.at[n], target)

        return do

    def rows_to(src, dst, me, n):
        def do(d, row, target):
            push(src.at[d], dst.at[me], a_send.at[n], a_recv.at[n], target)

        return do

    each_t(x, cy, z, keys_to(tk_out, tk_in, me_t, 1))
    each_s(x, cy, z, keys_to(sk_out, sk_in, me_s, 0))
    each_s(x, cy, z, rows_to(s_rows, s_all.at[z], me_s, 3))
    each_t(x, cy, z, rows_to(t_rows, t_all.at[x], me_t, 4))
    for n, src, dst in (
        (0, sk_out.at[x], sk_in.at[me_s]),
        (1, tk_out.at[z], tk_in.at[me_t]),
        (2, rk_out.at[lax.div(z, 2)], rk_in.at[me_r]),
        (3, s_rows.at[me_s], s_all.at[z, me_s]),
        (4, t_rows.at[me_t], t_all.at[x, me_t]),
    ):
        pltpu.make_async_copy(src, dst, a_recv.at[n]).start()

    each_r(x, core, y, z, keys_to(rk_out, rk_in, me_r, 2))

    started = []

    def ring(step, way, half):
        at = s_all.at[lax.rem(z + 8 - way * step, 8), pl.ds(16 * half, 16)]
        lane = 0 if way == 1 else 1
        started.append(push(
            at, at, ring_send.at[lane, step, half], ring_recv.at[lane, step, half],
            dev(x, core, y, lax.rem(z + 8 + way, 8)),
        ))

    def relay(step, way, last=False):
        at = lax.rem(z + 8 - way * (step + 1), 8)
        for half in range(2):
            drain(
                s_all.at[at, pl.ds(16 * half, 16)],
                ring_recv.at[0 if way == 1 else 1, step, half],
            )
            if not last:
                ring(step + 1, way, half)
        return at

    def x_half(block, half, way, n):
        part = t_all.at[block, pl.ds(32 * half, 32)]
        started.append(push(
            part, part, t_send.at[n], t_recv.at[n], dev(lax.rem(x + 4 + way, 4), core, y, z)
        ))

    def x_in(block, half, n):
        drain(t_all.at[block, pl.ds(32 * half, 32)], t_recv.at[n])

    drain(s_all.at[z], a_recv.at[3])
    for half in range(2):
        ring(0, 1, half)
        ring(0, -1, half)
    drain(tk_in, a_recv.at[1])
    pack_keys(tk_in, me_t, tk_all.at[x])
    for o in (2, 1, 3):
        started.append(push(
            tk_all.at[x], tk_all.at[x], tg_send.at[o - 1], tg_recv.at[o - 1],
            dev(lax.rem(x + o, 4), core, y, z),
        ))
    drain(sk_in, a_recv.at[0])
    pack_keys(sk_in, me_s, sk_all.at[z])
    for o in (4, 3, 5, 2, 6, 1, 7):
        started.append(push(
            sk_all.at[z], sk_all.at[z], sg_send.at[o - 1], sg_recv.at[o - 1],
            dev(x, core, y, lax.rem(z + o, 8)),
        ))
    one, two = relay(0, 1), relay(0, -1)
    drain(t_all.at[x], a_recv.at[4])
    x_half(x, 0, 1, 0)
    x_half(x, 1, -1, 1)
    x_half(x, 1, 1, 2)
    x_half(x, 0, -1, 3)
    drain(rk_in, a_recv.at[2])
    pack_keys(rk_in, me_r, rk_all.at[cy])
    for o in range(1, 8):
        d = lax.rem(cy + o, 8)
        started.append(push(
            rk_all.at[cy], rk_all.at[cy], rg_send.at[o - 1], rg_recv.at[o - 1],
            dev(x, lax.div(d, 4), lax.rem(d, 4), z),
        ))
    for o in range(1, 4):
        drain(tk_all.at[lax.rem(x + 4 - o, 4)], tg_recv.at[o - 1])
    for o in range(1, 8):
        drain(sk_all.at[lax.rem(z + 8 - o, 8)], sg_recv.at[o - 1])

    def count_s(i, total):
        kv = key_line(sk_all, i, 0)
        return total + last_dims(hot(kv >> 6), hot(kv & 63))

    def count_t(i, total):
        for half in range(2):
            kv = key_line(tk_all, i, 4 * half)
            total = total + last_dims(hot(kv >> 6), hot(kv & 63))
        return total

    zero = jnp.zeros((KEYS, KEYS), F32)
    sc = lax.fori_loop(0, 8, count_s, zero)
    tc = lax.fori_loop(0, 4, count_t, zero)
    both[0] = sc
    both[1] = tc

    def low(cnt):
        return cnt - jnp.floor(cnt * (1.0 / 256.0)) * 256.0

    s_share, t_share = low(tc).astype(BF16), low(sc).astype(BF16)

    def do_s(first, second):
        spots = (first, second)
        kv = jnp.concatenate([key_line(sk_all, at, 0) for at in spots], axis=1)
        product(
            kv, s_share,
            lambda r: s_all[spots[r // 4], 8 * (r % 4):8 * (r % 4) + 8].reshape(128, W),
            acc_s, lhs, rhs,
        )

    def do_t(at):
        kv = jnp.concatenate([key_line(tk_all, at, 0), key_line(tk_all, at, 4)], axis=1)
        product(
            kv, t_share, lambda r: t_all[at, 8 * r:8 * r + 8].reshape(128, W), acc_t, lhs, rhs
        )

    do_s(z, one)
    three, four = relay(1, 1), relay(1, -1)
    do_s(two, three)
    do_t(x)
    before, after, far = lax.rem(x + 3, 4), lax.rem(x + 1, 4), lax.rem(x + 2, 4)
    x_in(before, 0, 0)
    x_half(before, 0, 1, 4)
    x_in(after, 1, 1)
    x_half(after, 1, -1, 5)
    five, six = relay(2, 1), relay(2, -1, True)
    do_s(four, five)
    x_in(before, 1, 2)
    do_t(before)
    x_in(after, 0, 3)
    do_t(after)
    do_s(six, relay(3, 1, True))
    x_in(far, 0, 4)
    x_in(far, 1, 5)
    do_t(far)

    for o in range(1, 8):
        drain(rk_all.at[lax.rem(cy + 8 - o, 8)], rg_recv.at[o - 1])
    for n, ref in enumerate((sk_in, tk_in, rk_in)):
        drain(ref.at[pl.ds(0, ref.shape[0] - 1)], a_send.at[n])
    for n, ref in ((3, s_rows), (4, t_rows)):
        drain(ref.at[pl.ds(0, ref.shape[0] - 1)], a_send.at[n])
    for c in started:
        c.wait_send()


def dispatch(*args):
    vm = pl.BlockSpec(memory_space=pltpu.VMEM)
    dma = pltpu.SemaphoreType.DMA
    i32 = jnp.int32
    out = (
        jax.ShapeDtypeStruct((4096, W), F32),
        jax.ShapeDtypeStruct((4096, W), F32),
        jax.ShapeDtypeStruct((8, 32, CAP, W), BF16),
        jax.ShapeDtypeStruct((4, 64, CAP, W), BF16),
        jax.ShapeDtypeStruct((8, 8, 128), i32),
        jax.ShapeDtypeStruct((4, 8, 128), i32),
        jax.ShapeDtypeStruct((8, 8, 128), i32),
        jax.ShapeDtypeStruct((2, KEYS, KEYS), F32),
    )
    return pl.pallas_call(
        dispatch_kernel,
        out_shape=out,
        in_specs=[pl.BlockSpec(memory_space=pltpu.HBM)] * 8,
        out_specs=(vm,) * 8,
        scratch_shapes=[
            pltpu.VMEM((4, 128), i32), pltpu.VMEM((8, 128), i32), pltpu.VMEM((4, 128), i32),
            pltpu.VMEM((1, 32), i32), pltpu.VMEM((1, 64), i32), pltpu.VMEM((1, 32), i32),
            pltpu.VMEM((4, 1, 128), i32), pltpu.VMEM((8, 1, 128), i32), pltpu.VMEM((4, 1, 128), i32),
            pltpu.VMEM((32, 1, 128), i32), pltpu.VMEM((64, 1, 128), i32), pltpu.VMEM((32, 1, 128), i32),
            pltpu.VMEM((1024, 2 * CHUNK), BF16),
            pltpu.VMEM((2 * CHUNK, 4 * W), BF16),
            dma((6,)),
            dma((5,)), dma((5,)),
            dma((2, 4, 2)), dma((2, 4, 2)),
            dma((6,)), dma((6,)),
            dma((7,)), dma((7,)),
            dma((3,)), dma((3,)),
            dma((7,)), dma((7,)),
        ],
        compiler_params=pltpu.CompilerParams(
            collective_id=0, has_side_effects=True, vmem_limit_bytes=24 << 20
        ),
        name="dispatch",
    )(*(pltpu.with_memory_space_constraint(a, pltpu.HBM) for a in args))


def repair_kernel(
    both, sk_all, tk_all, s_all, t_all, was_s, was_t, acc_s, acc_t, block, table, lhs, rhs, sem
):
    @pl.when(jnp.max(both[...]) >= 256.0)
    def _():
        def high(cnt):
            return (jnp.floor(cnt * (1.0 / 256.0)) * 256.0).astype(BF16)

        def move(src, dst):
            copy = pltpu.make_async_copy(src, dst, sem)
            copy.start()
            copy.wait()

        def load(r):
            return block[8 * r:8 * r + 8].reshape(128, W)

        s_share, t_share = high(both[1]), high(both[0])

        def one_s(i, carry):
            move(s_all.at[i], block)
            product(key_line(sk_all, i, 0), s_share, load, table, lhs, rhs)
            return carry

        def one_t(i, carry):
            for half in range(2):
                move(t_all.at[i, pl.ds(32 * half, 32)], block)
                product(key_line(tk_all, i, 4 * half), t_share, load, table, lhs, rhs)
            return carry

        move(was_s, table)
        lax.fori_loop(0, 8, one_s, 0)
        move(table, acc_s)
        move(was_t, table)
        lax.fori_loop(0, 4, one_t, 0)
        move(table, acc_t)


def repair(both, sk_all, tk_all, s_all, t_all, acc_s, acc_t):
    hbm = pl.BlockSpec(memory_space=pl.ANY)
    vm = pl.BlockSpec(memory_space=pltpu.VMEM)
    total = jax.ShapeDtypeStruct((4096, W), F32)
    return pl.pallas_call(
        repair_kernel,
        out_shape=(total, total),
        in_specs=[vm, vm, vm, hbm, hbm, hbm, hbm],
        out_specs=(hbm, hbm),
        input_output_aliases={5: 0, 6: 1},
        scratch_shapes=[
            pltpu.VMEM((32, CAP, W), BF16),
            pltpu.VMEM((4096, W), F32),
            pltpu.VMEM((1024, CHUNK), BF16),
            pltpu.VMEM((CHUNK, 4 * W), BF16),
            pltpu.SemaphoreType.DMA,
        ],
        compiler_params=pltpu.CompilerParams(vmem_limit_bytes=24 << 20),
        name="repair",
    )(both, sk_all, tk_all, s_all, t_all, acc_s, acc_t)


def finish_kernel(
    at_s, at_t, acc_s, acc_t, rk_all, both, r_rows, out,
    away, ra, rb, h, scales, rows, joined, sems, p_send, p_recv, y_send, y_recv,
):
    x, core, y, z = place()
    me_r = z * 4 + x
    barrier = pltpu.get_barrier_semaphore()
    pl.semaphore_signal(barrier, inc=1, device_id=dev(x, 1 - core, y, z), device_id_type=MESH)
    for o in (1, 2, 3):
        pl.semaphore_signal(
            barrier, inc=1, device_id=dev(x, core, lax.rem(y + o, 4), z), device_id_type=MESH
        )
    each_r(x, core, y, z, greet(barrier))

    tri = last_dims(both[0], both[1], precision=lax.Precision.HIGHEST)
    stack = jnp.concatenate(split3(tri), axis=1)

    def lines(o, to):
        kv = jnp.concatenate([rk_all[o, r:r + 1, :] for r in range(4)], axis=1) - 1
        first = hot(kv >> 6)
        sums = jnp.dot(
            stack, jnp.concatenate([first, first, first], axis=0), preferred_element_type=F32
        )
        line = jnp.sum(sums * hot(kv & 63).astype(F32), axis=0, keepdims=True)
        for r in range(4):
            to[512 + r:513 + r, :] = line[:, 128 * r:128 * r + 128]
        to[516:520, :] = jnp.zeros((4, 128), F32)

    def gather(o, to):
        def some(i, carry):
            for u in range(16):
                n = o * 512 + i * 16 + u
                to[pl.ds(i * 16 + u, 1), :] = (
                    acc_s[pl.ds(at_s[n], 1), :] + acc_t[pl.ds(at_t[n], 1), :]
                )
            return carry

        lax.fori_loop(0, 32, some, 0)

    up, down = dev(x, core, lax.rem(y + 1, 4), z), dev(x, core, lax.rem(y + 3, 4), z)
    top, low = pl.ds(0, HALF_G), pl.ds(HALF_G, ROWS_G - HALF_G)

    def theirs(o):
        return (1 - core) * 4 + lax.rem(y + o, 4)

    def mine(o):
        return core * 4 + lax.rem(y + o, 4)

    def spread(d, row, target):
        push(r_rows.at[d], rows.at[me_r], sems.at[2], sems.at[3], target)

    partner, sent = {}, []

    def to_partner(o):
        partner[o] = push(
            away.at[o], ra.at[o], p_send.at[o], p_recv.at[o], dev(x, 1 - core, y, z)
        )

    def meet(o):
        partner[o].wait_recv()
        h[o] = h[o] + ra[o]

    def to_y(src, dst, n, target):
        sent.append(push(src, dst, y_send.at[n], y_recv.at[n], target))

    def both_lines(o, carry):
        lines(theirs(o), away.at[o])
        lines(mine(o), h.at[o])
        return carry

    gather(theirs(2), away.at[2])
    lax.fori_loop(0, 4, both_lines, 0)
    gather(mine(2), h.at[2])
    gather(theirs(1), away.at[1])
    pl.semaphore_wait(barrier, 1 + 3 + 31)
    to_partner(2)
    to_partner(1)
    gather(theirs(3), away.at[3])
    to_partner(3)
    meet(2)
    to_y(h.at[2, top], rb.at[2, top], 0, up)
    to_y(h.at[2, low], rb.at[2, low], 1, down)
    gather(mine(1), h.at[1])
    meet(1)
    to_y(h.at[1, low], rb.at[0, low], 2, up)
    gather(mine(3), h.at[3])
    meet(3)
    to_y(h.at[3, top], rb.at[1, top], 3, down)
    gather(theirs(0), away.at[0])
    to_partner(0)
    drain(rb.at[2, top], y_recv.at[0])
    h[1, top, :] = h[1, top, :] + rb[2, top, :]
    to_y(h.at[1, top], rb.at[0, top], 4, up)
    drain(rb.at[2, low], y_recv.at[1])
    h[3, low, :] = h[3, low, :] + rb[2, low, :]
    to_y(h.at[3, low], rb.at[1, low], 5, down)
    pltpu.make_async_copy(r_rows.at[me_r], rows.at[me_r], sems.at[3]).start()
    each_r(x, core, y, z, spread)
    gather(mine(0), h.at[0])
    meet(0)
    drain(rows, sems.at[3])
    for n, part in ((2, rb.at[0, low]), (3, rb.at[1, top]), (4, rb.at[0, top]), (5, rb.at[1, low])):
        drain(part, y_recv.at[n])
    line = h[0, 512:516, :] + rb[0, 512:516, :] + rb[1, 512:516, :]
    scale = jnp.where(rk_all[core * 4 + y, 0:4, :] > 0, 1.0 / jnp.sqrt(1.0 + line), 0.0)
    scales[...] = scale
    pair = lax.div(z, 2)
    xs = around(x, 4)
    for k in (2, 1, 3, 0):
        r = lax.rem(pair + k, 4)
        at = pl.ds(pl.multiple_of(128 * r, 128), 128)
        spot = pl.ds(8 * r, 8)
        side = jnp.transpose(jnp.broadcast_to(scales[pl.ds(r, 1), :], (128, 128)))
        total = h[0, at, :] + rb[0, at, :] + rb[1, at, :]
        value = rows[spot].reshape(128, W).astype(F32) * total * side
        joined[spot] = value.astype(BF16).reshape(8, CAP, W)
        for zz in (4 * r + 1 - z, z) if k == 0 else (2 * r, 2 * r + 1):
            for n, xx in enumerate(xs):
                d = zz * 4 + xx
                if k == 0 and zz is z and n == 0:
                    pltpu.make_async_copy(joined.at[d], out.at[me_r], sems.at[1]).start()
                else:
                    push(
                        joined.at[d], out.at[me_r], sems.at[0], sems.at[1], dev(xx, core, y, zz)
                    )
    drain(out, sems.at[1])
    drain(joined.at[pl.ds(0, 31)], sems.at[0])
    drain(rows.at[pl.ds(0, 31)], sems.at[2])
    for c in list(partner.values()) + sent:
        c.wait_send()


def finish(at_s, at_t, acc_s, acc_t, rk_all, both, r_rows):
    vm = pl.BlockSpec(memory_space=pltpu.VMEM)
    hbm = pl.BlockSpec(memory_space=pltpu.HBM)
    dma = pltpu.SemaphoreType.DMA
    return pl.pallas_call(
        finish_kernel,
        out_shape=jax.ShapeDtypeStruct((32, CAP, W), BF16),
        in_specs=[pl.BlockSpec(memory_space=pltpu.SMEM)] * 2 + [vm] * 4 + [hbm],
        out_specs=hbm,
        scratch_shapes=[
            pltpu.VMEM((4, ROWS_G, W), F32),
            pltpu.VMEM((4, ROWS_G, W), F32),
            pltpu.VMEM((3, ROWS_G, W), F32),
            pltpu.VMEM((4, ROWS_G, W), F32),
            pltpu.VMEM((4, 128), F32),
            pltpu.VMEM((32, CAP, W), BF16),
            pltpu.VMEM((32, CAP, W), BF16),
            dma((4,)), dma((4,)), dma((4,)), dma((6,)), dma((6,)),
        ],
        compiler_params=pltpu.CompilerParams(
            collective_id=1, has_side_effects=True, vmem_limit_bytes=24 << 20
        ),
        name="finish",
    )(at_s, at_t, acc_s, acc_t, rk_all, both, pltpu.with_memory_space_constraint(r_rows, pltpu.HBM))


def body(r_rows, r_keys, r_counts, s_rows, s_keys, s_counts, t_rows, t_keys, t_counts):
    acc_s, acc_t, s_all, t_all, sk_all, tk_all, rk_all, both = dispatch(
        s_rows.reshape(32, CAP, W), s_keys.reshape(4, 128), s_counts.reshape(1, 32),
        t_rows.reshape(64, CAP, W), t_keys.reshape(8, 128), t_counts.reshape(1, 64),
        r_keys.reshape(4, 128), r_counts.reshape(1, 32),
    )
    acc_s, acc_t = repair(both, sk_all, tk_all, s_all, t_all, acc_s, acc_t)
    kv = jnp.maximum(rk_all[:, :4] - 1, 0)
    a, b = kv >> 6, kv & 63
    at_s = (b & 3) * 1024 + (b >> 2) * 64 + a
    at_t = (a & 3) * 1024 + (a >> 2) * 64 + b
    joined = finish(at_s.reshape(4096), at_t.reshape(4096), acc_s, acc_t, rk_all, both, r_rows.reshape(32, CAP, W))
    return joined.reshape(512, W)


def solution(mesh):
    rows, line = P(("aa", "ba", "col"), None), P(("aa", "ba", "col"))
    return jax.shard_map(
        body, mesh=mesh, in_specs=(rows, line, line) * 3, out_specs=rows, check_vma=False
    )
```
